1024 devices in a mesh: ctx: 128 (over z, x, core), head: 8 (over y).
Axes of the slice: x: 4, y: 8, z: 16, core: 2. Of those that a mesh axis runs over, the one named last changes fastest.
Arguments:
- tokens: bfloat16 [32768, 4096], P('ctx', 'head'), may hold values from -6 to 6
- w_qkv: bfloat16 [4096, 3, 2048], P(None, None, 'head'), may hold values from -0.09375 to 0.09375
- log_gate: float32 [32768, 16], P('ctx', 'head'), may hold values from -1.1 to 0, as said below
- w_out: bfloat16 [2048, 4096], P(None, 'head'), may hold values from -0.125 to 0.125
Outputs:
- mixed: bfloat16 [32768, 4096], P('ctx', 'head')
The draws below stay inside these ranges and needn't reach their ends.
Inputs may be any that keep to these rules, and one draw needn't show every extreme that they name: `log_gate`: never positive.
All inputs are finite; a program needn't handle non-finite values.
Results may differ from the reference program's by a relative error of at most 0.013.
Values may be sent and summed in bfloat16 or wider, within the bound.
A program may use at most 64 MiB of HBM per device.

```python
import math
import jax
import jax.numpy as jnp
from jax import lax

D = 4096
SHARD_ATTN_NUM = 16
DH = 128
TOK_DEV = 256
CONTEXT_SLOTS = 32768
N_CTX = 128


def draw_log_gate(key, part):
    keyed_vectors = jax.random.split(key, 5)
    fast_rate = jnp.exp(jax.random.uniform(keyed_vectors[0], (SHARD_ATTN_NUM,), jnp.float32, math.log(1.0 / 200.0), math.log(1.0 / 180.0)))
    slow_rate = 0.4 * math.log(10.0) / CONTEXT_SLOTS
    share = 0.5
    is_fast = jax.random.uniform(keyed_vectors[1], (SHARD_ATTN_NUM,), jnp.float32) < share
    starting_shift = jnp.where(is_fast, fast_rate, slow_rate)
    forget_multiplier = jnp.exp(jax.random.uniform(keyed_vectors[2], (CONTEXT_SLOTS, SHARD_ATTN_NUM), jnp.float32, math.log(0.5), math.log(2.0)))
    segment_index = jax.random.randint(keyed_vectors[3], (2, SHARD_ATTN_NUM), 0, CONTEXT_SLOTS)
    learning_objective = jax.random.uniform(keyed_vectors[4], (2, SHARD_ATTN_NUM), jnp.float32, 0.2, 0.4)
    time_indices = jnp.arange(CONTEXT_SLOTS)[:, None]
    segment_span = jnp.where(time_indices == segment_index[0][None, :], jnp.log(1.0 - learning_objective[0])[None, :], 0.0)
    segment_span = segment_span + jnp.where(time_indices == segment_index[1][None, :], jnp.log(1.0 - learning_objective[1])[None, :], 0.0)
    return (-starting_shift[None, :] * forget_multiplier + segment_span).astype(jnp.float32)


def shard_levels(own_key, dims, cuts, smallest, high):
    def one(position, shards_of):
        steps = jax.random.uniform(jax.random.fold_in(jax.random.fold_in(own_key, 6), position), (shards_of,), jnp.float32, smallest / len(cuts), high / len(cuts))
        return jnp.repeat(jnp.exp(steps), dims[position] // shards_of).reshape((-1,) + (1,) * (len(dims) - position - 1))

    gain = one(*cuts[0])
    for cut in cuts[1:]:
        gain = gain * one(*cut)
    return gain


def gaussian(own_key, shape, spread, reach, cuts=(), kind=jnp.bfloat16):
    factor_of = shard_levels(own_key, shape, cuts, -0.22, 0.18) if cuts else 1.0
    values = jax.random.normal(own_key, shape, jnp.float32) * spread * factor_of
    return jnp.minimum(jnp.maximum(values, -reach), reach).astype(kind)


def setup_inputs(seed: int = 0) -> dict:
    seeds = jax.random.split(jax.random.key(seed), 5)
    tokens = gaussian(seeds[0], (CONTEXT_SLOTS, D), 1.0, 6.0, ((0, 128), (1, 8)))
    w_qkv = gaussian(seeds[1], (D, 3, SHARD_ATTN_NUM * DH), D ** -0.5, 0.09375, ((2, 8),))
    log_gate = draw_log_gate(jax.random.fold_in(seeds[4], 71), 0)
    w_out = gaussian(seeds[3], (SHARD_ATTN_NUM * DH, D), (SHARD_ATTN_NUM * DH) ** -0.5, 0.125, ((1, 8),))
    return dict(tokens=tokens, w_qkv=w_qkv, log_gate=log_gate, w_out=w_out)


def reference(tokens, w_qkv, log_gate, w_out):
    width = SHARD_ATTN_NUM * DH
    flat_w = w_qkv.reshape(D, 3 * width)
    scale = DH ** (-0.5)
    tok_blocks = tokens.reshape(N_CTX, TOK_DEV, D)
    gate_blocks = log_gate.reshape(N_CTX, TOK_DEV, SHARD_ATTN_NUM)
    causal = jnp.tril(jnp.ones((TOK_DEV, TOK_DEV), dtype=bool))

    def step(state, inputs):
        block, gates = inputs
        qkv = jnp.dot(block, flat_w, preferred_element_type=jnp.float32).astype(jnp.bfloat16)
        qkv = qkv.reshape(TOK_DEV, 3, SHARD_ATTN_NUM, DH)
        query = qkv[:, 0].astype(jnp.float32)
        keyed_vectors = qkv[:, 1].astype(jnp.float32)
        values = qkv[:, 2].astype(jnp.float32)
        cumul = jnp.cumsum(gates, axis=0)
        cumul_t = cumul.T
        diff = cumul_t[:, :, None] - cumul_t[:, None, :]
        decay = jnp.where(causal[None], jnp.exp(jnp.where(causal[None], diff, 0.0)), 0.0)
        scores = jnp.einsum('thd,shd->hts', query, keyed_vectors) * scale
        weights = (scores * decay).astype(jnp.bfloat16).astype(jnp.float32)
        intra = jnp.einsum('hts,shd->thd', weights, values)
        scaled_q = query * (scale * jnp.exp(cumul))[:, :, None]
        inter = jnp.einsum('thd,hde->the', scaled_q, state, precision=lax.Precision.HIGHEST)
        attn = intra + inter
        normed = attn * lax.rsqrt(lax.optimization_barrier(jnp.mean(attn * attn, axis=-1, keepdims=True)) + 1e-06)
        normed = normed.astype(jnp.bfloat16).reshape(TOK_DEV, width)
        out_block = jnp.dot(normed, w_out, preferred_element_type=jnp.float32).astype(jnp.bfloat16)
        last = cumul[-1]
        keep = jnp.exp(last[None, :] - cumul)
        weighted_k = keyed_vectors * keep[:, :, None]
        local = jnp.einsum('thd,the->hde', weighted_k, values, precision=lax.Precision.HIGHEST)
        state = jnp.exp(last)[:, None, None] * state + local
        return (state, out_block)
    start = jnp.zeros((SHARD_ATTN_NUM, DH, DH), jnp.float32)
    final, outs = lax.scan(step, start, (tok_blocks, gate_blocks))
    return outs.reshape(CONTEXT_SLOTS, D)
```

```python
import functools

import jax
import jax.numpy as jnp
from jax import lax
from jax.experimental import pallas as pl
from jax.experimental.pallas import tpu as pltpu
from jax.sharding import PartitionSpec as P

DH = 128
PLANE = 8
HEADS = 2
MESH = pl.DeviceIdType.MESH
F32 = jnp.float32
BF16 = jnp.bfloat16


def kernel(
    NY, NZ, tok_hbm, w_hbm, gate_ref, wout_hbm, out_ref,
    tok_buf, w_buf, wout_buf, acc, k_buf, v_buf, dec_buf, keep_buf, eb_buf, intra_buf,
    n_buf, oacc, s_buf, sp_buf, pre_buf, t_send, t_recv, st_send, st_recv,
    l_send, lp_buf, lz_send, lz_recv, wz_buf,
    w_sem, wout_sem, own_sem, tsend, trecv, nsend, nrecv,
    zh, ph, lps, lpr, lzs, lzr, sps, spr, tzs, tzr, sts, strv,
):
    ctx = lax.axis_index("ctx")
    y = lax.axis_index("head")
    z, j = ctx // PLANE, ctx % PLANE
    x, core = j // 2, j % 2
    feat = tok_hbm.shape[1]
    rows = tok_hbm.shape[0]
    half_rows = rows // 2
    scale = DH ** (-0.5)

    right, left = (y + 1) % NY, (y + NY - 1) % NY
    jxr = ((x + 1) % 4) * 2 + core
    jxl = ((x + 3) % 4) * 2 + core
    jcore = x * 2 + (1 - core)
    zr = ((z + 1) % NZ) * PLANE + j
    zl = ((z + NZ - 1) % NZ) * PLANE + j
    base = z * PLANE

    own = pltpu.make_async_copy(tok_hbm, tok_buf.at[y], own_sem)
    own.start()
    w_copy = pltpu.make_async_copy(w_hbm, w_buf, w_sem)
    w_copy.start()
    wout_copy = pltpu.make_async_copy(wout_hbm, wout_buf, wout_sem)

    barrier = pltpu.get_barrier_semaphore()
    for dev in ((ctx, right), (ctx, left), (base + jxr, y), (base + jxl, y), (base + jcore, y), (zr, y), (zl, y)):
        pl.semaphore_signal(barrier, inc=1, device_id=dev, device_id_type=MESH)
    pl.semaphore_wait(barrier, 7)

    far = NY // 2
    near = NY - 1 - far

    def ring_copy(src, buf, ssem, rsem, d, half, s, slot):
        to = jnp.where(d == 0, right, left)
        part = pl.ds(pl.multiple_of(half * half_rows, half_rows), half_rows)
        return pltpu.make_async_remote_copy(
            src_ref=src.at[part], dst_ref=buf.at[slot, part],
            send_sem=ssem.at[d, half, s], recv_sem=rsem.at[d, half, s],
            device_id=(ctx, to), device_id_type=MESH,
        )

    def origin(d, s):
        return jnp.where(d == 0, y + NY - s, y + s) % NY

    def ring_start(src, buf, ssem, rsem):
        for d, half in ((0, 0), (1, 1), (0, 1), (1, 0)):
            if (d == half) or near > 0:
                ring_copy(src, buf, ssem, rsem, d, half, 0, y).start()

    def ring_take(buf, ssem, rsem, d, half, s):
        slot = origin(d, s)
        ring_copy(buf.at[slot], buf, ssem, rsem, d, half, s - 1, slot).wait_recv()
        return slot

    def ring_drain(src, buf, ssem, rsem):
        for d, half in ((0, 0), (1, 1), (0, 1), (1, 0)):
            for s in range(far if d == half else near):
                ring_copy(src, buf, ssem, rsem, d, half, s, y).wait_send()

    ring_start(tok_hbm, tok_buf, tsend, trecv)
    wout_copy.start()

    def z_hello(r):
        pl.semaphore_signal(zh.at[0, r], inc=1, device_id=(zr, y), device_id_type=MESH)
        pl.semaphore_signal(zh.at[1, r], inc=1, device_id=(zl, y), device_id_type=MESH)

    def plane_hello(r):
        pl.semaphore_signal(ph.at[r, 0], inc=1, device_id=(base + jxr, y), device_id_type=MESH)
        pl.semaphore_signal(ph.at[r, 1], inc=1, device_id=(base + jxl, y), device_id_type=MESH)
        pl.semaphore_signal(ph.at[r, 2], inc=1, device_id=(base + jcore, y), device_id_type=MESH)

    def plane_heard(r):
        for q in range(3):
            pl.semaphore_wait(ph.at[r, q], 1)

    steps = 4 * near
    z_rounds = NZ // 2 - 1
    z_hello(0)
    plane_hello(0)

    rid = lax.broadcasted_iota(jnp.int32, (rows, rows), 0)
    cid = lax.broadcasted_iota(jnp.int32, (rows, rows), 1)
    causal = cid <= rid
    for h in range(HEADS):
        g_row = gate_ref[h : h + 1, :]
        b_col = jnp.sum(jnp.where(causal, g_row, 0.0), axis=1, keepdims=True)
        b_row = jnp.sum(jnp.where(cid == rid, b_col, 0.0), axis=0, keepdims=True)
        last = b_col[rows - 1 : rows, :]
        diff = jnp.where(causal, b_col - b_row, 0.0)
        dec_buf[h] = jnp.where(causal, jnp.exp(diff) * scale, 0.0)
        keep_buf[h] = jnp.broadcast_to(jnp.exp(last - b_col), (rows, DH))
        eb_buf[h] = jnp.broadcast_to(jnp.exp(b_col) * scale, (rows, DH))
        l_send[h] = jnp.broadcast_to(last, (8, DH))

    def plane_copy(src, dst, ssem, rsem, d):
        to = (j + d) % PLANE
        return pltpu.make_async_remote_copy(
            src_ref=src(to), dst_ref=dst.at[j], send_sem=ssem.at[d], recv_sem=rsem.at[d],
            device_id=(base + to, y), device_id_type=MESH,
        )

    def l_copy(d):
        return plane_copy(lambda to: l_send.at[to // 4], lp_buf, lps, lpr, d)

    def s_copy(d):
        return plane_copy(lambda to: s_buf.at[to], sp_buf, sps, spr, d)

    def st_copy(d):
        return plane_copy(lambda to: st_send.at[to], st_recv, sts, strv, d)

    def z_copy(src, dst, ssem, rsem, k):
        return pltpu.make_async_remote_copy(
            src_ref=src, dst_ref=dst.at[k], send_sem=ssem.at[k], recv_sem=rsem.at[k],
            device_id=((ctx + PLANE * k) % (PLANE * NZ), y), device_id_type=MESH,
        )

    z_order = sorted(range(1, NZ), key=lambda k: -min(k, NZ - k))

    own.wait()
    w_copy.wait()

    def project(part, slot, half):
        r = pl.ds(pl.multiple_of(half * half_rows, half_rows), half_rows)
        f = pl.ds(pl.multiple_of(slot * feat, feat), feat)
        return jnp.dot(tok_buf[slot, r, :], w_buf[part, f, :], preferred_element_type=F32)

    for part in range(3):
        f = pl.ds(pl.multiple_of(y * feat, feat), feat)
        acc[part] = jnp.dot(tok_buf[y], w_buf[part, f, :], preferred_element_type=F32)

    def token_step(i, carry):
        s, ci = i // 4 + 1, i % 4
        d, half = ci % 2, (ci + ci // 2) % 2
        slot = ring_take(tok_buf, tsend, trecv, d, half, s)

        @pl.when(jnp.logical_or(d == half, s < near))
        def _():
            ring_copy(tok_buf.at[slot], tok_buf, tsend, trecv, d, half, s, slot).start()

        r = pl.ds(pl.multiple_of(half * half_rows, half_rows), half_rows)
        for part in range(3):
            acc[part, r, :] = acc[part, r, :] + project(part, slot, half)

        @pl.when(i < z_rounds)
        def _():
            pl.semaphore_wait(zh.at[0, i], 1)
            pl.semaphore_wait(zh.at[1, i], 1)

        @pl.when(i + 1 < z_rounds)
        def _():
            z_hello(i + 1)

        @pl.when(i == 0)
        def _():
            plane_heard(0)
            plane_hello(1)

        @pl.when(i == 1)
        def _():
            plane_heard(1)
            for q in range(1, PLANE):
                l_copy(q).start()
            lp_buf[j] = l_send[j // 4]

        @pl.when(i == min(7, steps - 1))
        def _():
            for q in range(1, PLANE):
                l_copy(q).wait()
            total = lp_buf[0]
            for b in range(1, PLANE):
                total = total + lp_buf[b]
            lz_send[...] = total
            for k in z_order:
                @pl.when(z + k < NZ)
                def _():
                    z_copy(lz_send, lz_recv, lzs, lzr, k).start()

        return carry

    lax.fori_loop(0, steps, token_step, 0)

    run = jnp.zeros((8, DH), F32)
    for k in range(1, NZ):
        wz_buf[k] = jnp.exp(run)

        @pl.when(z >= k)
        def _():
            z_copy(lz_send, lz_recv, lzs, lzr, k).wait_recv()

        @pl.when(z < k)
        def _():
            lz_recv[k] = jnp.zeros((8, DH), F32)

        run = run + lz_recv[k]

    ring_take(tok_buf, tsend, trecv, 0, 0, far)
    slot = ring_take(tok_buf, tsend, trecv, 1, 1, far)
    f = pl.ds(pl.multiple_of(slot * feat, feat), feat)

    def finish(part):
        return (acc[part] + jnp.dot(tok_buf[slot], w_buf[part, f, :], preferred_element_type=F32)).astype(BF16)

    k_buf[...] = finish(1)
    v_buf[...] = finish(2)
    per = PLANE // HEADS
    seg = DH // per
    for h in range(HEADS):
        cols = slice(h * DH, (h + 1) * DH)
        weighted = (k_buf[:, cols].astype(F32) * keep_buf[h]).astype(BF16)
        local = lax.dot_general(weighted, v_buf[:, cols], (((0,), (0,)), ((), ())), preferred_element_type=F32)
        s_buf[h * per : (h + 1) * per] = local.astype(BF16).reshape(per, seg, DH)
    for q in range(1, PLANE):
        s_copy(q).start()
    sp_buf[j] = s_buf[j]

    query = finish(0)
    for h in range(HEADS):
        cols = slice(h * DH, (h + 1) * DH)
        scores = lax.dot_general(query[:, cols], k_buf[:, cols], (((1,), (1,)), ((), ())), preferred_element_type=F32)
        weights = (scores * dec_buf[h]).astype(BF16)
        intra_buf[h] = jnp.dot(weights, v_buf[:, cols], preferred_element_type=F32)

    for q in range(1, PLANE):
        s_copy(q).wait_recv()
    state = jnp.zeros((seg, DH), F32)
    gone = jnp.zeros((8, DH), F32)
    for b in range(PLANE):
        pre_buf[b] = state
        log_b = jnp.concatenate([lp_buf[b]] * (seg // 8), axis=0)
        state = jnp.exp(log_b) * state + sp_buf[b].astype(F32)
    t_send[...] = state.astype(BF16)
    for k in z_order:
        @pl.when(z + k < NZ)
        def _():
            z_copy(t_send, t_recv, tzs, tzr, k).start()

    pre_buf[PLANE] = jnp.zeros((seg, DH), F32)
    for k in range(1, NZ):
        @pl.when(z >= k)
        def _():
            z_copy(t_send, t_recv, tzs, tzr, k).wait_recv()
            w_k = jnp.concatenate([wz_buf[k]] * (seg // 8), axis=0)
            pre_buf[PLANE] = pre_buf[PLANE] + w_k * t_recv[k].astype(F32)

    before = pre_buf[PLANE]
    for b in range(PLANE):
        gone_b = jnp.concatenate([jnp.exp(gone)] * (seg // 8), axis=0)
        st_send[b] = (gone_b * before + pre_buf[b]).astype(BF16)
        gone = gone + lp_buf[b]
    for q in range(1, PLANE):
        st_copy(q).start()
    st_recv[j] = st_send[j]
    for q in range(1, PLANE):
        st_copy(q).wait_recv()

    for h in range(HEADS):
        cols = slice(h * DH, (h + 1) * DH)
        prev = st_recv[h * per : (h + 1) * per].reshape(DH, DH)
        inter = jnp.dot(query[:, cols], prev, preferred_element_type=F32) * eb_buf[h]
        attn = intra_buf[h] + inter
        normed = attn * lax.rsqrt(jnp.mean(attn * attn, axis=1, keepdims=True) + 1e-6)
        n_buf[y, :, cols] = normed.astype(BF16)

    ring_start(n_buf.at[y], n_buf, nsend, nrecv)
    width = HEADS * DH
    wout_copy.wait()
    f = pl.ds(pl.multiple_of(y * width, width), width)
    oacc[...] = jnp.dot(n_buf[y], wout_buf[f, :], preferred_element_type=F32)

    def out_step(i, carry):
        s, ci = i // 4 + 1, i % 4
        d, half = ci % 2, (ci + ci // 2) % 2
        slot = ring_take(n_buf, nsend, nrecv, d, half, s)

        @pl.when(jnp.logical_or(d == half, s < near))
        def _():
            ring_copy(n_buf.at[slot], n_buf, nsend, nrecv, d, half, s, slot).start()

        r = pl.ds(pl.multiple_of(half * half_rows, half_rows), half_rows)
        f = pl.ds(pl.multiple_of(slot * width, width), width)
        oacc[r, :] = oacc[r, :] + jnp.dot(n_buf[slot, r, :], wout_buf[f, :], preferred_element_type=F32)
        return carry

    lax.fori_loop(0, steps, out_step, 0)
    ring_take(n_buf, nsend, nrecv, 0, 0, far)
    slot = ring_take(n_buf, nsend, nrecv, 1, 1, far)
    f = pl.ds(pl.multiple_of(slot * width, width), width)
    out_ref[...] = (oacc[...] + jnp.dot(n_buf[slot], wout_buf[f, :], preferred_element_type=F32)).astype(BF16)

    ring_drain(tok_hbm, tok_buf, tsend, trecv)
    ring_drain(n_buf.at[y], n_buf, nsend, nrecv)
    for q in range(1, PLANE):
        s_copy(q).wait_send()
        st_copy(q).wait_send()
    for k in range(1, NZ):
        @pl.when(z + k < NZ)
        def _():
            z_copy(lz_send, lz_recv, lzs, lzr, k).wait_send()
            z_copy(t_send, t_recv, tzs, tzr, k).wait_send()


def body(NY, NZ, tokens, w_qkv, log_gate, w_out):
    rows, feat = tokens.shape
    width = HEADS * DH
    seg = HEADS * DH // PLANE
    dma = pltpu.SemaphoreType.DMA
    far = NY // 2
    any_spec = pl.BlockSpec(memory_space=pl.ANY)
    vmem_spec = pl.BlockSpec(memory_space=pltpu.VMEM)
    w3 = jnp.transpose(w_qkv, (1, 0, 2))
    gates = jnp.transpose(log_gate, (1, 0))
    scratch = [
        pltpu.VMEM((NY, rows, feat), BF16),
        pltpu.VMEM(w3.shape, BF16),
        pltpu.VMEM(w_out.shape, BF16),
        pltpu.VMEM((3, rows, width), F32),
        pltpu.VMEM((rows, width), BF16),
        pltpu.VMEM((rows, width), BF16),
        pltpu.VMEM((HEADS, rows, rows), F32),
        pltpu.VMEM((HEADS, rows, DH), F32),
        pltpu.VMEM((HEADS, rows, DH), F32),
        pltpu.VMEM((HEADS, rows, DH), F32),
        pltpu.VMEM((NY, rows, width), BF16),
        pltpu.VMEM((rows, w_out.shape[1]), F32),
        pltpu.VMEM((PLANE, seg, DH), BF16),
        pltpu.VMEM((PLANE, seg, DH), BF16),
        pltpu.VMEM((PLANE + 1, seg, DH), F32),
        pltpu.VMEM((seg, DH), BF16),
        pltpu.VMEM((NZ, seg, DH), BF16),
        pltpu.VMEM((PLANE, seg, DH), BF16),
        pltpu.VMEM((PLANE, seg, DH), BF16),
        pltpu.VMEM((HEADS, 8, DH), F32),
        pltpu.VMEM((PLANE, 8, DH), F32),
        pltpu.VMEM((8, DH), F32),
        pltpu.VMEM((NZ, 8, DH), F32),
        pltpu.VMEM((NZ, 8, DH), F32),
        dma, dma, dma,
        dma((2, 2, far)), dma((2, 2, far)), dma((2, 2, far)), dma((2, 2, far)),
        pltpu.SemaphoreType.REGULAR((2, max(NZ // 2 - 1, 1))),
        pltpu.SemaphoreType.REGULAR((2, 3)),
        dma((PLANE,)), dma((PLANE,)),
        dma((NZ,)), dma((NZ,)),
        dma((PLANE,)), dma((PLANE,)),
        dma((NZ,)), dma((NZ,)),
        dma((PLANE,)), dma((PLANE,)),
    ]
    return pl.pallas_call(
        functools.partial(kernel, NY, NZ),
        out_shape=jax.ShapeDtypeStruct((rows, w_out.shape[1]), BF16),
        in_specs=[any_spec, any_spec, vmem_spec, any_spec],
        out_specs=vmem_spec,
        scratch_shapes=scratch,
        compiler_params=pltpu.CompilerParams(
            collective_id=0, has_side_effects=True, vmem_limit_bytes=40 << 20
        ),
    )(tokens, w3, gates, w_out)


def solution(mesh):
    placed = (P("ctx", "head"), P(None, None, "head"), P("ctx", "head"), P(None, "head"))
    return jax.shard_map(
        functools.partial(body, mesh.shape["head"], mesh.shape["ctx"] // PLANE),
        mesh=mesh, in_specs=placed, out_specs=P("ctx", "head"), check_vma=False,
    )
```

```python
import functools

import jax
import jax.numpy as jnp
from jax import lax
from jax.experimental import pallas as pl
from jax.experimental.pallas import tpu as pltpu
from jax.sharding import PartitionSpec as P

DH = 128
PLANE = 8
HEADS = 2
MESH = pl.DeviceIdType.MESH
F32 = jnp.float32
BF16 = jnp.bfloat16


def kernel(
    NY, NZ, tok_hbm, w_hbm, gate_ref, wout_hbm, out_ref,
    tok_buf, w_buf, wout_buf, acc, k_buf, v_buf, dec_buf, keep_buf, eb_buf, intra_buf,
    n_buf, oacc, s_buf, sp_buf, pre_buf, t_send, t_recv, st_send, st_recv,
    l_send, lp_buf, lz_send, lz_recv, wz_buf,
    w_sem, wout_sem, own_sem, tsend, trecv, nsend, nrecv,
    zh, ph, lps, lpr, lzs, lzr, sps, spr, tzs, tzr, sts, strv,
):
    ctx = lax.axis_index("ctx")
    y = lax.axis_index("head")
    z, j = ctx // PLANE, ctx % PLANE
    x, core = j // 2, j % 2
    feat = tok_hbm.shape[1]
    rows = tok_hbm.shape[0]
    half_rows = rows // 2
    scale = DH ** (-0.5)

    right, left = (y + 1) % NY, (y + NY - 1) % NY
    jxr = ((x + 1) % 4) * 2 + core
    jxl = ((x + 3) % 4) * 2 + core
    jcore = x * 2 + (1 - core)
    zr = ((z + 1) % NZ) * PLANE + j
    zl = ((z + NZ - 1) % NZ) * PLANE + j
    base = z * PLANE

    own = pltpu.make_async_copy(tok_hbm, tok_buf.at[y], own_sem)
    own.start()
    w_copy = pltpu.make_async_copy(w_hbm, w_buf, w_sem)
    w_copy.start()
    wout_copy = pltpu.make_async_copy(wout_hbm, wout_buf, wout_sem)

    barrier = pltpu.get_barrier_semaphore()
    for dev in ((ctx, right), (ctx, left), (base + jxr, y), (base + jxl, y), (base + jcore, y), (zr, y), (zl, y)):
        pl.semaphore_signal(barrier, inc=1, device_id=dev, device_id_type=MESH)
    with jax.named_scope("entry"):
        pl.semaphore_wait(barrier, 7)

    far = NY // 2
    near = NY - 1 - far

    def ring_copy(src, buf, ssem, rsem, d, half, s, slot):
        to = jnp.where(d == 0, right, left)
        part = pl.ds(pl.multiple_of(half * half_rows, half_rows), half_rows)
        return pltpu.make_async_remote_copy(
            src_ref=src.at[part], dst_ref=buf.at[slot, part],
            send_sem=ssem.at[d, half, s], recv_sem=rsem.at[d, half, s],
            device_id=(ctx, to), device_id_type=MESH,
        )

    def origin(d, s):
        return jnp.where(d == 0, y + NY - s, y + s) % NY

    def ring_start(src, buf, ssem, rsem):
        for d, half in ((0, 0), (1, 1), (0, 1), (1, 0)):
            if (d == half) or near > 0:
                ring_copy(src, buf, ssem, rsem, d, half, 0, y).start()

    def ring_take(buf, ssem, rsem, d, half, s):
        slot = origin(d, s)
        ring_copy(buf.at[slot], buf, ssem, rsem, d, half, s - 1, slot).wait_recv()
        return slot

    def ring_drain(src, buf, ssem, rsem):
        for d, half in ((0, 0), (1, 1), (0, 1), (1, 0)):
            for s in range(far if d == half else near):
                ring_copy(src, buf, ssem, rsem, d, half, s, y).wait_send()

    ring_start(tok_hbm, tok_buf, tsend, trecv)
    wout_copy.start()

    def z_hello(r):
        pl.semaphore_signal(zh.at[0, r], inc=1, device_id=(zr, y), device_id_type=MESH)
        pl.semaphore_signal(zh.at[1, r], inc=1, device_id=(zl, y), device_id_type=MESH)

    def plane_hello(r):
        pl.semaphore_signal(ph.at[r, 0], inc=1, device_id=(base + jxr, y), device_id_type=MESH)
        pl.semaphore_signal(ph.at[r, 1], inc=1, device_id=(base + jxl, y), device_id_type=MESH)
        pl.semaphore_signal(ph.at[r, 2], inc=1, device_id=(base + jcore, y), device_id_type=MESH)

    def plane_heard(r):
        for q in range(3):
            pl.semaphore_wait(ph.at[r, q], 1)

    steps = 4 * near
    z_rounds = NZ // 2 - 1
    z_hello(0)
    plane_hello(0)

    with jax.named_scope("gates"):
        rid = lax.broadcasted_iota(jnp.int32, (rows, rows), 0)
        cid = lax.broadcasted_iota(jnp.int32, (rows, rows), 1)
        causal = cid <= rid
        for h in range(HEADS):
            g_row = gate_ref[h : h + 1, :]
            b_col = jnp.sum(jnp.where(causal, g_row, 0.0), axis=1, keepdims=True)
            b_row = jnp.sum(jnp.where(cid == rid, b_col, 0.0), axis=0, keepdims=True)
            last = b_col[rows - 1 : rows, :]
            diff = jnp.where(causal, b_col - b_row, 0.0)
            dec_buf[h] = jnp.where(causal, jnp.exp(diff) * scale, 0.0)
            keep_buf[h] = jnp.broadcast_to(jnp.exp(last - b_col), (rows, DH))
            eb_buf[h] = jnp.broadcast_to(jnp.exp(b_col) * scale, (rows, DH))
            l_send[h] = jnp.broadcast_to(last, (8, DH))

    def plane_copy(src, dst, ssem, rsem, d):
        to = (j + d) % PLANE
        return pltpu.make_async_remote_copy(
            src_ref=src(to), dst_ref=dst.at[j], send_sem=ssem.at[d], recv_sem=rsem.at[d],
            device_id=(base + to, y), device_id_type=MESH,
        )

    def l_copy(d):
        return plane_copy(lambda to: l_send.at[to // 4], lp_buf, lps, lpr, d)

    def s_copy(d):
        return plane_copy(lambda to: s_buf.at[to], sp_buf, sps, spr, d)

    def st_copy(d):
        return plane_copy(lambda to: st_send.at[to], st_recv, sts, strv, d)

    def z_copy(src, dst, ssem, rsem, k):
        return pltpu.make_async_remote_copy(
            src_ref=src, dst_ref=dst.at[k], send_sem=ssem.at[k], recv_sem=rsem.at[k],
            device_id=((ctx + PLANE * k) % (PLANE * NZ), y), device_id_type=MESH,
        )

    z_order = sorted(range(1, NZ), key=lambda k: -min(k, NZ - k))

    with jax.named_scope("loads"):
        own.wait()
        w_copy.wait()

    def project(part, slot, half):
        r = pl.ds(pl.multiple_of(half * half_rows, half_rows), half_rows)
        f = pl.ds(pl.multiple_of(slot * feat, feat), feat)
        return jnp.dot(tok_buf[slot, r, :], w_buf[part, f, :], preferred_element_type=F32)

    for part in range(3):
        f = pl.ds(pl.multiple_of(y * feat, feat), feat)
        acc[part] = jnp.dot(tok_buf[y], w_buf[part, f, :], preferred_element_type=F32)

    def token_step(i, carry):
        s, ci = i // 4 + 1, i % 4
        d, half = ci % 2, (ci + ci // 2) % 2
        slot = ring_take(tok_buf, tsend, trecv, d, half, s)

        @pl.when(jnp.logical_or(d == half, s < near))
        def _():
            ring_copy(tok_buf.at[slot], tok_buf, tsend, trecv, d, half, s, slot).start()

        r = pl.ds(pl.multiple_of(half * half_rows, half_rows), half_rows)
        for part in range(3):
            acc[part, r, :] = acc[part, r, :] + project(part, slot, half)

        @pl.when(i < z_rounds)
        def _():
            pl.semaphore_wait(zh.at[0, i], 1)
            pl.semaphore_wait(zh.at[1, i], 1)

        @pl.when(i + 1 < z_rounds)
        def _():
            z_hello(i + 1)

        @pl.when(i == 0)
        def _():
            plane_heard(0)
            plane_hello(1)

        @pl.when(i == 1)
        def _():
            plane_heard(1)
            for q in range(1, PLANE):
                l_copy(q).start()
            lp_buf[j] = l_send[j // 4]

        @pl.when(i == min(7, steps - 1))
        def _():
            for q in range(1, PLANE):
                l_copy(q).wait()
            total = lp_buf[0]
            for b in range(1, PLANE):
                total = total + lp_buf[b]
            lz_send[...] = total
            for k in z_order:
                @pl.when(z + k < NZ)
                def _():
                    z_copy(lz_send, lz_recv, lzs, lzr, k).start()

        return carry

    with jax.named_scope("token_ring"):
        lax.fori_loop(0, steps, token_step, 0)

    with jax.named_scope("plane_weights"):
        run = jnp.zeros((8, DH), F32)
        for k in range(1, NZ):
            wz_buf[k] = jnp.exp(run)

            @pl.when(z >= k)
            def _():
                z_copy(lz_send, lz_recv, lzs, lzr, k).wait_recv()

            @pl.when(z < k)
            def _():
                lz_recv[k] = jnp.zeros((8, DH), F32)

            run = run + lz_recv[k]

    with jax.named_scope("token_last"):
        ring_take(tok_buf, tsend, trecv, 0, 0, far)
        slot = ring_take(tok_buf, tsend, trecv, 1, 1, far)
        f = pl.ds(pl.multiple_of(slot * feat, feat), feat)

        def finish(part):
            return (acc[part] + jnp.dot(tok_buf[slot], w_buf[part, f, :], preferred_element_type=F32)).astype(BF16)

    with jax.named_scope("local_state"):
        k_buf[...] = finish(1)
        v_buf[...] = finish(2)
        per = PLANE // HEADS
        seg = DH // per
        for h in range(HEADS):
            cols = slice(h * DH, (h + 1) * DH)
            weighted = (k_buf[:, cols].astype(F32) * keep_buf[h]).astype(BF16)
            local = lax.dot_general(weighted, v_buf[:, cols], (((0,), (0,)), ((), ())), preferred_element_type=F32)
            s_buf[h * per : (h + 1) * per] = local.astype(BF16).reshape(per, seg, DH)
        for q in range(1, PLANE):
            s_copy(q).start()
        sp_buf[j] = s_buf[j]

    with jax.named_scope("intra"):
        query = finish(0)
        for h in range(HEADS):
            cols = slice(h * DH, (h + 1) * DH)
            scores = lax.dot_general(query[:, cols], k_buf[:, cols], (((1,), (1,)), ((), ())), preferred_element_type=F32)
            weights = (scores * dec_buf[h]).astype(BF16)
            intra_buf[h] = jnp.dot(weights, v_buf[:, cols], preferred_element_type=F32)

    with jax.named_scope("plane_totals"):
        for q in range(1, PLANE):
            s_copy(q).wait_recv()
        state = jnp.zeros((seg, DH), F32)
        gone = jnp.zeros((8, DH), F32)
        for b in range(PLANE):
            pre_buf[b] = state
            log_b = jnp.concatenate([lp_buf[b]] * (seg // 8), axis=0)
            state = jnp.exp(log_b) * state + sp_buf[b].astype(F32)
        t_send[...] = state.astype(BF16)
        for k in z_order:
            @pl.when(z + k < NZ)
            def _():
                z_copy(t_send, t_recv, tzs, tzr, k).start()

    with jax.named_scope("earlier_planes"):
        pre_buf[PLANE] = jnp.zeros((seg, DH), F32)
        for k in range(1, NZ):
            @pl.when(z >= k)
            def _():
                z_copy(t_send, t_recv, tzs, tzr, k).wait_recv()
                w_k = jnp.concatenate([wz_buf[k]] * (seg // 8), axis=0)
                pre_buf[PLANE] = pre_buf[PLANE] + w_k * t_recv[k].astype(F32)

    with jax.named_scope("prefixes"):
        before = pre_buf[PLANE]
        for b in range(PLANE):
            gone_b = jnp.concatenate([jnp.exp(gone)] * (seg // 8), axis=0)
            st_send[b] = (gone_b * before + pre_buf[b]).astype(BF16)
            gone = gone + lp_buf[b]
        for q in range(1, PLANE):
            st_copy(q).start()
        st_recv[j] = st_send[j]
        for q in range(1, PLANE):
            st_copy(q).wait_recv()

    with jax.named_scope("normed"):
        for h in range(HEADS):
            cols = slice(h * DH, (h + 1) * DH)
            prev = st_recv[h * per : (h + 1) * per].reshape(DH, DH)
            inter = jnp.dot(query[:, cols], prev, preferred_element_type=F32) * eb_buf[h]
            attn = intra_buf[h] + inter
            normed = attn * lax.rsqrt(jnp.mean(attn * attn, axis=1, keepdims=True) + 1e-6)
            n_buf[y, :, cols] = normed.astype(BF16)

    ring_start(n_buf.at[y], n_buf, nsend, nrecv)
    width = HEADS * DH
    wout_copy.wait()
    f = pl.ds(pl.multiple_of(y * width, width), width)
    oacc[...] = jnp.dot(n_buf[y], wout_buf[f, :], preferred_element_type=F32)

    def out_step(i, carry):
        s, ci = i // 4 + 1, i % 4
        d, half = ci % 2, (ci + ci // 2) % 2
        slot = ring_take(n_buf, nsend, nrecv, d, half, s)

        @pl.when(jnp.logical_or(d == half, s < near))
        def _():
            ring_copy(n_buf.at[slot], n_buf, nsend, nrecv, d, half, s, slot).start()

        r = pl.ds(pl.multiple_of(half * half_rows, half_rows), half_rows)
        f = pl.ds(pl.multiple_of(slot * width, width), width)
        oacc[r, :] = oacc[r, :] + jnp.dot(n_buf[slot, r, :], wout_buf[f, :], preferred_element_type=F32)
        return carry

    with jax.named_scope("out_ring"):
        lax.fori_loop(0, steps, out_step, 0)
    with jax.named_scope("out_last"):
        ring_take(n_buf, nsend, nrecv, 0, 0, far)
        slot = ring_take(n_buf, nsend, nrecv, 1, 1, far)
        f = pl.ds(pl.multiple_of(slot * width, width), width)
        out_ref[...] = (oacc[...] + jnp.dot(n_buf[slot], wout_buf[f, :], preferred_element_type=F32)).astype(BF16)

    with jax.named_scope("drain"):
        ring_drain(tok_hbm, tok_buf, tsend, trecv)
        ring_drain(n_buf.at[y], n_buf, nsend, nrecv)
        for q in range(1, PLANE):
            s_copy(q).wait_send()
            st_copy(q).wait_send()
        for k in range(1, NZ):
            @pl.when(z + k < NZ)
            def _():
                z_copy(lz_send, lz_recv, lzs, lzr, k).wait_send()
                z_copy(t_send, t_recv, tzs, tzr, k).wait_send()


def body(NY, NZ, tokens, w_qkv, log_gate, w_out):
    rows, feat = tokens.shape
    width = HEADS * DH
    seg = HEADS * DH // PLANE
    dma = pltpu.SemaphoreType.DMA
    far = NY // 2
    any_spec = pl.BlockSpec(memory_space=pl.ANY)
    vmem_spec = pl.BlockSpec(memory_space=pltpu.VMEM)
    w3 = jnp.transpose(w_qkv, (1, 0, 2))
    gates = jnp.transpose(log_gate, (1, 0))
    scratch = [
        pltpu.VMEM((NY, rows, feat), BF16),
        pltpu.VMEM(w3.shape, BF16),
        pltpu.VMEM(w_out.shape, BF16),
        pltpu.VMEM((3, rows, width), F32),
        pltpu.VMEM((rows, width), BF16),
        pltpu.VMEM((rows, width), BF16),
        pltpu.VMEM((HEADS, rows, rows), F32),
        pltpu.VMEM((HEADS, rows, DH), F32),
        pltpu.VMEM((HEADS, rows, DH), F32),
        pltpu.VMEM((HEADS, rows, DH), F32),
        pltpu.VMEM((NY, rows, width), BF16),
        pltpu.VMEM((rows, w_out.shape[1]), F32),
        pltpu.VMEM((PLANE, seg, DH), BF16),
        pltpu.VMEM((PLANE, seg, DH), BF16),
        pltpu.VMEM((PLANE + 1, seg, DH), F32),
        pltpu.VMEM((seg, DH), BF16),
        pltpu.VMEM((NZ, seg, DH), BF16),
        pltpu.VMEM((PLANE, seg, DH), BF16),
        pltpu.VMEM((PLANE, seg, DH), BF16),
        pltpu.VMEM((HEADS, 8, DH), F32),
        pltpu.VMEM((PLANE, 8, DH), F32),
        pltpu.VMEM((8, DH), F32),
        pltpu.VMEM((NZ, 8, DH), F32),
        pltpu.VMEM((NZ, 8, DH), F32),
        dma, dma, dma,
        dma((2, 2, far)), dma((2, 2, far)), dma((2, 2, far)), dma((2, 2, far)),
        pltpu.SemaphoreType.REGULAR((2, max(NZ // 2 - 1, 1))),
        pltpu.SemaphoreType.REGULAR((2, 3)),
        dma((PLANE,)), dma((PLANE,)),
        dma((NZ,)), dma((NZ,)),
        dma((PLANE,)), dma((PLANE,)),
        dma((NZ,)), dma((NZ,)),
        dma((PLANE,)), dma((PLANE,)),
    ]
    return pl.pallas_call(
        functools.partial(kernel, NY, NZ),
        out_shape=jax.ShapeDtypeStruct((rows, w_out.shape[1]), BF16),
        in_specs=[any_spec, any_spec, vmem_spec, any_spec],
        out_specs=vmem_spec,
        scratch_shapes=scratch,
        compiler_params=pltpu.CompilerParams(
            collective_id=0, has_side_effects=True, vmem_limit_bytes=63 << 20
        ),
    )(tokens, w3, gates, w_out)


def solution(mesh):
    placed = (P("ctx", "head"), P(None, None, "head"), P("ctx", "head"), P(None, "head"))
    return jax.shard_map(
        functools.partial(body, mesh.shape["head"], mesh.shape["ctx"] // PLANE),
        mesh=mesh, in_specs=placed, out_specs=P("ctx", "head"), check_vma=False,
    )
```

```python
import functools

import jax
import jax.numpy as jnp
from jax import lax
from jax.experimental import pallas as pl
from jax.experimental.pallas import tpu as pltpu
from jax.sharding import PartitionSpec as P

DH = 128
PLANE = 8
HEADS = 2
MESH = pl.DeviceIdType.MESH
F32 = jnp.float32
BF16 = jnp.bfloat16


def kernel(
    NY, NZ, tok_hbm, w_hbm, gate_ref, wout_hbm, out_ref,
    tok_buf, w_buf, wout_buf, acc, k_buf, v_buf, dec_buf, keep_buf, eb_buf, intra_buf,
    n_buf, oacc, s_buf, sp_buf, pre_buf, t_send, t_recv, st_send, st_recv,
    l_send, lp_buf, lz_send, lz_recv, wz_buf,
    w_sem, wout_sem, own_sem, tsend, trecv, nsend, nrecv,
    zh, ph, relay, lps, lpr, lzs, lzr, sps, spr, tzs, tzr, sts, strv,
):
    ctx = lax.axis_index("ctx")
    y = lax.axis_index("head")
    z, j = ctx // PLANE, ctx % PLANE
    x, core = j // 2, j % 2
    feat = tok_hbm.shape[1]
    rows = tok_hbm.shape[0]
    half_rows = rows // 2
    scale = DH ** (-0.5)

    right, left = (y + 1) % NY, (y + NY - 1) % NY
    jxr = ((x + 1) % 4) * 2 + core
    jxl = ((x + 3) % 4) * 2 + core
    jcore = x * 2 + (1 - core)
    zr = ((z + 1) % NZ) * PLANE + j
    zl = ((z + NZ - 1) % NZ) * PLANE + j
    base = z * PLANE

    own = pltpu.make_async_copy(tok_hbm, tok_buf.at[y], own_sem)
    own.start()
    w_copy = pltpu.make_async_copy(w_hbm, w_buf, w_sem)
    w_copy.start()
    wout_copy = pltpu.make_async_copy(wout_hbm, wout_buf, wout_sem)

    barrier = pltpu.get_barrier_semaphore()
    for dev in ((ctx, right), (ctx, left)):
        pl.semaphore_signal(barrier, inc=1, device_id=dev, device_id_type=MESH)

    @pl.when(y > 0)
    def _():
        for dev in (base + jxr, base + jxl, base + jcore, zl):
            pl.semaphore_signal(barrier, inc=1, device_id=(dev, y), device_id_type=MESH)

    with jax.named_scope("entry"):
        @pl.when(y > 0)
        def _():
            pl.semaphore_wait(barrier, 6)

        @pl.when(y == 0)
        def _():
            pl.semaphore_wait(barrier, 2)

    far = NY // 2
    near = NY - 1 - far

    def ring_copy(src, buf, ssem, rsem, d, half, s, slot):
        to = jnp.where(d == 0, right, left)
        part = pl.ds(pl.multiple_of(half * half_rows, half_rows), half_rows)
        return pltpu.make_async_remote_copy(
            src_ref=src.at[part], dst_ref=buf.at[slot, part],
            send_sem=ssem.at[d, half, s], recv_sem=rsem.at[d, half, s],
            device_id=(ctx, to), device_id_type=MESH,
        )

    def origin(d, s):
        return jnp.where(d == 0, y + NY - s, y + s) % NY

    def ring_start(src, buf, ssem, rsem):
        for d, half in ((0, 0), (1, 1), (0, 1), (1, 0)):
            if (d == half) or near > 0:
                ring_copy(src, buf, ssem, rsem, d, half, 0, y).start()

    def ring_take(buf, ssem, rsem, d, half, s):
        slot = origin(d, s)
        ring_copy(buf.at[slot], buf, ssem, rsem, d, half, s - 1, slot).wait_recv()
        return slot

    def ring_drain(src, buf, ssem, rsem):
        for d, half in ((0, 0), (1, 1), (0, 1), (1, 0)):
            for s in range(far if d == half else near):
                ring_copy(src, buf, ssem, rsem, d, half, s, y).wait_send()

    ring_start(tok_hbm, tok_buf, tsend, trecv)
    wout_copy.start()

    steps = 4 * near
    up_rounds, down_rounds = NZ // 2, NZ // 2 - 1
    up_from = jnp.maximum(0, jnp.minimum(4, 3 * NZ // 4 - z))
    down_from = 5

    def hello_up(r):
        pl.semaphore_signal(zh.at[0, r], inc=1, device_id=(zr, y), device_id_type=MESH)

    def hello_down(r):
        pl.semaphore_signal(zh.at[1, r], inc=1, device_id=(zl, y), device_id_type=MESH)

    def plane_hello(r):
        pl.semaphore_signal(ph.at[r, 0], inc=1, device_id=(base + jxr, y), device_id_type=MESH)
        pl.semaphore_signal(ph.at[r, 1], inc=1, device_id=(base + jxl, y), device_id_type=MESH)
        pl.semaphore_signal(ph.at[r, 2], inc=1, device_id=(base + jcore, y), device_id_type=MESH)

    def plane_heard(r):
        for q in range(3):
            pl.semaphore_wait(ph.at[r, q], 1)

    def tell_first_row(r):
        @pl.when(y == 1)
        def _():
            pl.semaphore_signal(relay.at[r], inc=1, device_id=(ctx, 0), device_id_type=MESH)

    def first_row_heard(r):
        @pl.when(y == 0)
        def _():
            pl.semaphore_wait(relay.at[r], 1)

    @pl.when(y > 0)
    def _():
        hello_up(0)
        plane_hello(0)

    with jax.named_scope("gates"):
        rid = lax.broadcasted_iota(jnp.int32, (rows, rows), 0)
        cid = lax.broadcasted_iota(jnp.int32, (rows, rows), 1)
        causal = cid <= rid
        for h in range(HEADS):
            g_row = gate_ref[h : h + 1, :]
            b_col = jnp.sum(jnp.where(causal, g_row, 0.0), axis=1, keepdims=True)
            b_row = jnp.sum(jnp.where(cid == rid, b_col, 0.0), axis=0, keepdims=True)
            last = b_col[rows - 1 : rows, :]
            diff = jnp.where(causal, b_col - b_row, 0.0)
            dec_buf[h] = jnp.where(causal, jnp.exp(diff) * scale, 0.0)
            keep_buf[h] = jnp.broadcast_to(jnp.exp(last - b_col), (rows, DH))
            eb_buf[h] = jnp.broadcast_to(jnp.exp(b_col) * scale, (rows, DH))
            l_send[h] = jnp.broadcast_to(last, (8, DH))

    def plane_copy(src, dst, ssem, rsem, d):
        to = (j + d) % PLANE
        return pltpu.make_async_remote_copy(
            src_ref=src(to), dst_ref=dst.at[j], send_sem=ssem.at[d], recv_sem=rsem.at[d],
            device_id=(base + to, y), device_id_type=MESH,
        )

    def l_copy(d):
        return plane_copy(lambda to: l_send.at[to // 4], lp_buf, lps, lpr, d)

    def s_copy(d):
        return plane_copy(lambda to: s_buf.at[to], sp_buf, sps, spr, d)

    def st_copy(d):
        return plane_copy(lambda to: st_send.at[to], st_recv, sts, strv, d)

    def z_copy(src, dst, ssem, rsem, k):
        return pltpu.make_async_remote_copy(
            src_ref=src, dst_ref=dst.at[k], send_sem=ssem.at[k], recv_sem=rsem.at[k],
            device_id=((ctx + PLANE * k) % (PLANE * NZ), y), device_id_type=MESH,
        )

    z_order = sorted(range(1, NZ), key=lambda k: -min(k, NZ - k))

    with jax.named_scope("loads"):
        own.wait()
        w_copy.wait()

    def project(part, slot, half):
        r = pl.ds(pl.multiple_of(half * half_rows, half_rows), half_rows)
        f = pl.ds(pl.multiple_of(slot * feat, feat), feat)
        return jnp.dot(tok_buf[slot, r, :], w_buf[part, f, :], preferred_element_type=F32)

    for part in range(3):
        f = pl.ds(pl.multiple_of(y * feat, feat), feat)
        acc[part] = jnp.dot(tok_buf[y], w_buf[part, f, :], preferred_element_type=F32)

    def token_step(i, carry):
        s, ci = i // 4 + 1, i % 4
        d, half = ci % 2, (ci + ci // 2) % 2
        slot = ring_take(tok_buf, tsend, trecv, d, half, s)

        @pl.when(jnp.logical_or(d == half, s < near))
        def _():
            ring_copy(tok_buf.at[slot], tok_buf, tsend, trecv, d, half, s, slot).start()

        r = pl.ds(pl.multiple_of(half * half_rows, half_rows), half_rows)
        for part in range(3):
            acc[part, r, :] = acc[part, r, :] + project(part, slot, half)

        @pl.when(y > 0)
        def _():
            up, down = i - up_from, i - down_from

            @pl.when(jnp.logical_and(up >= 0, up < up_rounds))
            def _():
                pl.semaphore_wait(zh.at[0, up], 1)

                @pl.when(up == 0)
                def _():
                    hello_down(0)

                @pl.when(up + 1 < up_rounds)
                def _():
                    hello_up(up + 1)

            @pl.when(jnp.logical_and(down >= 0, down < down_rounds))
            def _():
                pl.semaphore_wait(zh.at[1, down], 1)

                @pl.when(down + 1 < down_rounds)
                def _():
                    hello_down(down + 1)

            @pl.when(i == 3)
            def _():
                plane_heard(0)
                plane_hello(1)

            @pl.when(i == 5)
            def _():
                plane_heard(1)
                plane_hello(2)

            @pl.when(i == 7)
            def _():
                plane_heard(2)
                tell_first_row(0)

        @pl.when(i == 8)
        def _():
            first_row_heard(0)
            for q in range(1, PLANE):
                l_copy(q).start()
            lp_buf[j] = l_send[j // 4]

        return carry

    with jax.named_scope("token_ring"):
        lax.fori_loop(0, steps, token_step, 0)

    with jax.named_scope("plane_logs"):
        tell_first_row(1)
        first_row_heard(1)
        for q in range(1, PLANE):
            l_copy(q).wait()
        total = lp_buf[0]
        for b in range(1, PLANE):
            total = total + lp_buf[b]
        lz_send[...] = total
        for k in z_order:
            @pl.when(z + k < NZ)
            def _():
                z_copy(lz_send, lz_recv, lzs, lzr, k).start()

    with jax.named_scope("token_last"):
        ring_take(tok_buf, tsend, trecv, 0, 0, far)
        slot = ring_take(tok_buf, tsend, trecv, 1, 1, far)
        f = pl.ds(pl.multiple_of(slot * feat, feat), feat)

        def finish(part):
            return (acc[part] + jnp.dot(tok_buf[slot], w_buf[part, f, :], preferred_element_type=F32)).astype(BF16)

    with jax.named_scope("local_state"):
        k_buf[...] = finish(1)
        v_buf[...] = finish(2)
        per = PLANE // HEADS
        seg = DH // per
        for h in range(HEADS):
            cols = slice(h * DH, (h + 1) * DH)
            weighted = (k_buf[:, cols].astype(F32) * keep_buf[h]).astype(BF16)
            local = lax.dot_general(weighted, v_buf[:, cols], (((0,), (0,)), ((), ())), preferred_element_type=F32)
            s_buf[h * per : (h + 1) * per] = local.astype(BF16).reshape(per, seg, DH)
        for q in range(1, PLANE):
            s_copy(q).start()
        sp_buf[j] = s_buf[j]

    with jax.named_scope("intra"):
        query = finish(0)
        for h in range(HEADS):
            cols = slice(h * DH, (h + 1) * DH)
            scores = lax.dot_general(query[:, cols], k_buf[:, cols], (((1,), (1,)), ((), ())), preferred_element_type=F32)
            weights = (scores * dec_buf[h]).astype(BF16)
            intra_buf[h] = jnp.dot(weights, v_buf[:, cols], preferred_element_type=F32)

    with jax.named_scope("plane_totals"):
        for q in range(1, PLANE):
            s_copy(q).wait_recv()
        state = jnp.zeros((seg, DH), F32)
        gone = jnp.zeros((8, DH), F32)
        for b in range(PLANE):
            pre_buf[b] = state
            log_b = jnp.concatenate([lp_buf[b]] * (seg // 8), axis=0)
            state = jnp.exp(log_b) * state + sp_buf[b].astype(F32)
        t_send[...] = state.astype(BF16)
        for k in z_order:
            @pl.when(z + k < NZ)
            def _():
                z_copy(t_send, t_recv, tzs, tzr, k).start()

    with jax.named_scope("plane_weights"):
        run = jnp.zeros((8, DH), F32)
        for k in range(1, NZ):
            wz_buf[k] = jnp.exp(run)

            @pl.when(z >= k)
            def _():
                z_copy(lz_send, lz_recv, lzs, lzr, k).wait_recv()

            @pl.when(z < k)
            def _():
                lz_recv[k] = jnp.zeros((8, DH), F32)

            run = run + lz_recv[k]

    with jax.named_scope("earlier_planes"):
        pre_buf[PLANE] = jnp.zeros((seg, DH), F32)
        for k in range(1, NZ):
            @pl.when(z >= k)
            def _():
                z_copy(t_send, t_recv, tzs, tzr, k).wait_recv()
                w_k = jnp.concatenate([wz_buf[k]] * (seg // 8), axis=0)
                pre_buf[PLANE] = pre_buf[PLANE] + w_k * t_recv[k].astype(F32)

    with jax.named_scope("prefixes"):
        before = pre_buf[PLANE]
        for b in range(PLANE):
            gone_b = jnp.concatenate([jnp.exp(gone)] * (seg // 8), axis=0)
            st_send[b] = (gone_b * before + pre_buf[b]).astype(BF16)
            gone = gone + lp_buf[b]
        for q in range(1, PLANE):
            st_copy(q).start()
        st_recv[j] = st_send[j]
        for q in range(1, PLANE):
            st_copy(q).wait_recv()

    with jax.named_scope("normed"):
        for h in range(HEADS):
            cols = slice(h * DH, (h + 1) * DH)
            prev = st_recv[h * per : (h + 1) * per].reshape(DH, DH)
            inter = jnp.dot(query[:, cols], prev, preferred_element_type=F32) * eb_buf[h]
            attn = intra_buf[h] + inter
            normed = attn * lax.rsqrt(jnp.mean(attn * attn, axis=1, keepdims=True) + 1e-6)
            n_buf[y, :, cols] = normed.astype(BF16)

    ring_start(n_buf.at[y], n_buf, nsend, nrecv)
    width = HEADS * DH
    wout_copy.wait()
    f = pl.ds(pl.multiple_of(y * width, width), width)
    oacc[...] = jnp.dot(n_buf[y], wout_buf[f, :], preferred_element_type=F32)

    def out_step(i, carry):
        s, ci = i // 4 + 1, i % 4
        d, half = ci % 2, (ci + ci // 2) % 2
        slot = ring_take(n_buf, nsend, nrecv, d, half, s)

        @pl.when(jnp.logical_or(d == half, s < near))
        def _():
            ring_copy(n_buf.at[slot], n_buf, nsend, nrecv, d, half, s, slot).start()

        r = pl.ds(pl.multiple_of(half * half_rows, half_rows), half_rows)
        f = pl.ds(pl.multiple_of(slot * width, width), width)
        oacc[r, :] = oacc[r, :] + jnp.dot(n_buf[slot, r, :], wout_buf[f, :], preferred_element_type=F32)
        return carry

    with jax.named_scope("out_ring"):
        lax.fori_loop(0, steps, out_step, 0)
    with jax.named_scope("out_last"):
        ring_take(n_buf, nsend, nrecv, 0, 0, far)
        slot = ring_take(n_buf, nsend, nrecv, 1, 1, far)
        f = pl.ds(pl.multiple_of(slot * width, width), width)
        out_ref[...] = (oacc[...] + jnp.dot(n_buf[slot], wout_buf[f, :], preferred_element_type=F32)).astype(BF16)

    with jax.named_scope("drain"):
        ring_drain(tok_hbm, tok_buf, tsend, trecv)
        ring_drain(n_buf.at[y], n_buf, nsend, nrecv)
        for q in range(1, PLANE):
            s_copy(q).wait_send()
            st_copy(q).wait_send()
        for k in range(1, NZ):
            @pl.when(z + k < NZ)
            def _():
                z_copy(lz_send, lz_recv, lzs, lzr, k).wait_send()
                z_copy(t_send, t_recv, tzs, tzr, k).wait_send()


def body(NY, NZ, tokens, w_qkv, log_gate, w_out):
    rows, feat = tokens.shape
    width = HEADS * DH
    seg = HEADS * DH // PLANE
    dma = pltpu.SemaphoreType.DMA
    far = NY // 2
    any_spec = pl.BlockSpec(memory_space=pl.ANY)
    vmem_spec = pl.BlockSpec(memory_space=pltpu.VMEM)
    w3 = jnp.transpose(w_qkv, (1, 0, 2))
    gates = jnp.transpose(log_gate, (1, 0))
    scratch = [
        pltpu.VMEM((NY, rows, feat), BF16),
        pltpu.VMEM(w3.shape, BF16),
        pltpu.VMEM(w_out.shape, BF16),
        pltpu.VMEM((3, rows, width), F32),
        pltpu.VMEM((rows, width), BF16),
        pltpu.VMEM((rows, width), BF16),
        pltpu.VMEM((HEADS, rows, rows), F32),
        pltpu.VMEM((HEADS, rows, DH), F32),
        pltpu.VMEM((HEADS, rows, DH), F32),
        pltpu.VMEM((HEADS, rows, DH), F32),
        pltpu.VMEM((NY, rows, width), BF16),
        pltpu.VMEM((rows, w_out.shape[1]), F32),
        pltpu.VMEM((PLANE, seg, DH), BF16),
        pltpu.VMEM((PLANE, seg, DH), BF16),
        pltpu.VMEM((PLANE + 1, seg, DH), F32),
        pltpu.VMEM((seg, DH), BF16),
        pltpu.VMEM((NZ, seg, DH), BF16),
        pltpu.VMEM((PLANE, seg, DH), BF16),
        pltpu.VMEM((PLANE, seg, DH), BF16),
        pltpu.VMEM((HEADS, 8, DH), F32),
        pltpu.VMEM((PLANE, 8, DH), F32),
        pltpu.VMEM((8, DH), F32),
        pltpu.VMEM((NZ, 8, DH), F32),
        pltpu.VMEM((NZ, 8, DH), F32),
        dma, dma, dma,
        dma((2, 2, far)), dma((2, 2, far)), dma((2, 2, far)), dma((2, 2, far)),
        pltpu.SemaphoreType.REGULAR((2, NZ // 2)),
        pltpu.SemaphoreType.REGULAR((3, 3)),
        pltpu.SemaphoreType.REGULAR((2,)),
        dma((PLANE,)), dma((PLANE,)),
        dma((NZ,)), dma((NZ,)),
        dma((PLANE,)), dma((PLANE,)),
        dma((NZ,)), dma((NZ,)),
        dma((PLANE,)), dma((PLANE,)),
    ]
    return pl.pallas_call(
        functools.partial(kernel, NY, NZ),
        out_shape=jax.ShapeDtypeStruct((rows, w_out.shape[1]), BF16),
        in_specs=[any_spec, any_spec, vmem_spec, any_spec],
        out_specs=vmem_spec,
        scratch_shapes=scratch,
        compiler_params=pltpu.CompilerParams(
            collective_id=0, has_side_effects=True, vmem_limit_bytes=63 << 20
        ),
    )(tokens, w3, gates, w_out)


def solution(mesh):
    placed = (P("ctx", "head"), P(None, None, "head"), P("ctx", "head"), P(None, "head"))
    return jax.shard_map(
        functools.partial(body, mesh.shape["head"], mesh.shape["ctx"] // PLANE),
        mesh=mesh, in_specs=placed, out_specs=P("ctx", "head"), check_vma=False,
    )
```

```python
import functools

import jax
import jax.numpy as jnp
from jax import lax
from jax.experimental import pallas as pl
from jax.experimental.pallas import tpu as pltpu
from jax.sharding import PartitionSpec as P

DH = 128
PLANE = 8
HEADS = 2
MESH = pl.DeviceIdType.MESH
F32 = jnp.float32
BF16 = jnp.bfloat16


def kernel(
    NY, NZ, tok_hbm, w_hbm, gate_ref, wout_hbm, out_ref,
    tok_buf, w_buf, wout_buf, acc, k_buf, v_buf, dec_buf, keep_buf, eb_buf, intra_buf,
    n_buf, oacc, s_buf, sp_buf, pre_buf, t_send, t_recv, st_send, st_recv,
    l_send, lp_buf, lz_send, lz_recv, wz_buf,
    w_sem, wout_sem, own_sem, tsend, trecv, nsend, nrecv,
    before_in, later_in, ph, relay, lps, lpr, lzs, lzr, sps, spr, tzs, tzr, sts, strv,
):
    ctx = lax.axis_index("ctx")
    y = lax.axis_index("head")
    z, j = ctx // PLANE, ctx % PLANE
    x, core = j // 2, j % 2
    feat = tok_hbm.shape[1]
    rows = tok_hbm.shape[0]
    half_rows = rows // 2
    scale = DH ** (-0.5)

    right, left = (y + 1) % NY, (y + NY - 1) % NY
    jxr = ((x + 1) % 4) * 2 + core
    jxl = ((x + 3) % 4) * 2 + core
    jcore = x * 2 + (1 - core)
    base = z * PLANE

    own = pltpu.make_async_copy(tok_hbm, tok_buf.at[y], own_sem)
    own.start()
    w_copy = pltpu.make_async_copy(w_hbm, w_buf, w_sem)
    w_copy.start()
    wout_copy = pltpu.make_async_copy(wout_hbm, wout_buf, wout_sem)

    barrier = pltpu.get_barrier_semaphore()
    for dev in ((ctx, right), (ctx, left)):
        pl.semaphore_signal(barrier, inc=1, device_id=dev, device_id_type=MESH)

    @pl.when(y > 0)
    def _():
        for dev in (base + jxr, base + jxl, base + jcore):
            pl.semaphore_signal(barrier, inc=1, device_id=(dev, y), device_id_type=MESH)

        @pl.when(z > 0)
        def _():
            pl.semaphore_signal(barrier, inc=1, device_id=(ctx - PLANE, y), device_id_type=MESH)

    with jax.named_scope("entry"):
        pl.semaphore_wait(barrier, 2 + jnp.where(y > 0, 3, 0) + jnp.where(jnp.logical_and(y > 0, z < NZ - 1), 1, 0))

    far = NY // 2
    near = NY - 1 - far

    def ring_copy(src, buf, ssem, rsem, d, half, s, slot):
        to = jnp.where(d == 0, right, left)
        part = pl.ds(pl.multiple_of(half * half_rows, half_rows), half_rows)
        return pltpu.make_async_remote_copy(
            src_ref=src.at[part], dst_ref=buf.at[slot, part],
            send_sem=ssem.at[d, half, s], recv_sem=rsem.at[d, half, s],
            device_id=(ctx, to), device_id_type=MESH,
        )

    def origin(d, s):
        return jnp.where(d == 0, y + NY - s, y + s) % NY

    def ring_start(src, buf, ssem, rsem):
        for d, half in ((0, 0), (1, 1), (0, 1), (1, 0)):
            if (d == half) or near > 0:
                ring_copy(src, buf, ssem, rsem, d, half, 0, y).start()

    def ring_take(buf, ssem, rsem, d, half, s):
        slot = origin(d, s)
        ring_copy(buf.at[slot], buf, ssem, rsem, d, half, s - 1, slot).wait_recv()
        return slot

    def ring_drain(src, buf, ssem, rsem):
        for d, half in ((0, 0), (1, 1), (0, 1), (1, 0)):
            for s in range(far if d == half else near):
                ring_copy(src, buf, ssem, rsem, d, half, s, y).wait_send()

    ring_start(tok_hbm, tok_buf, tsend, trecv)
    wout_copy.start()

    steps = 4 * near
    chain_at = jnp.where(z >= NZ // 2, (NZ - 1 - z) // 2 + 1, 5 + (NZ // 2 - 1 - z) * 5 // 4)
    chain_at = jnp.minimum(chain_at, steps - 1)

    def chain_down():
        @pl.when(z < NZ - 1)
        def _():
            pl.semaphore_wait(later_in, 1)

        @pl.when(z > 0)
        def _():
            pl.semaphore_wait(before_in, 1)
            pl.semaphore_signal(later_in, inc=1, device_id=(ctx - PLANE, y), device_id_type=MESH)

    def plane_hello(r):
        pl.semaphore_signal(ph.at[r, 0], inc=1, device_id=(base + jxr, y), device_id_type=MESH)
        pl.semaphore_signal(ph.at[r, 1], inc=1, device_id=(base + jxl, y), device_id_type=MESH)
        pl.semaphore_signal(ph.at[r, 2], inc=1, device_id=(base + jcore, y), device_id_type=MESH)

    def plane_heard(r):
        for q in range(3):
            pl.semaphore_wait(ph.at[r, q], 1)

    def tell_first_row(r):
        @pl.when(y == 1)
        def _():
            pl.semaphore_signal(relay.at[r], inc=1, device_id=(ctx, 0), device_id_type=MESH)

    def first_row_heard(r):
        @pl.when(y == 0)
        def _():
            pl.semaphore_wait(relay.at[r], 1)

    @pl.when(y > 0)
    def _():
        plane_hello(0)

        @pl.when(z < NZ - 1)
        def _():
            pl.semaphore_signal(before_in, inc=1, device_id=(ctx + PLANE, y), device_id_type=MESH)

    with jax.named_scope("gates"):
        rid = lax.broadcasted_iota(jnp.int32, (rows, rows), 0)
        cid = lax.broadcasted_iota(jnp.int32, (rows, rows), 1)
        causal = cid <= rid
        for h in range(HEADS):
            g_row = gate_ref[h : h + 1, :]
            b_col = jnp.sum(jnp.where(causal, g_row, 0.0), axis=1, keepdims=True)
            b_row = jnp.sum(jnp.where(cid == rid, b_col, 0.0), axis=0, keepdims=True)
            last = b_col[rows - 1 : rows, :]
            diff = jnp.where(causal, b_col - b_row, 0.0)
            dec_buf[h] = jnp.where(causal, jnp.exp(diff) * scale, 0.0)
            keep_buf[h] = jnp.broadcast_to(jnp.exp(last - b_col), (rows, DH))
            eb_buf[h] = jnp.broadcast_to(jnp.exp(b_col) * scale, (rows, DH))
            l_send[h] = jnp.broadcast_to(last, (8, DH))

    def plane_copy(src, dst, ssem, rsem, d):
        to = (j + d) % PLANE
        return pltpu.make_async_remote_copy(
            src_ref=src(to), dst_ref=dst.at[j], send_sem=ssem.at[d], recv_sem=rsem.at[d],
            device_id=(base + to, y), device_id_type=MESH,
        )

    def l_copy(d):
        return plane_copy(lambda to: l_send.at[to // 4], lp_buf, lps, lpr, d)

    def s_copy(d):
        return plane_copy(lambda to: s_buf.at[to], sp_buf, sps, spr, d)

    def st_copy(d):
        return plane_copy(lambda to: st_send.at[to], st_recv, sts, strv, d)

    def z_copy(src, dst, ssem, rsem, k):
        return pltpu.make_async_remote_copy(
            src_ref=src, dst_ref=dst.at[k], send_sem=ssem.at[k], recv_sem=rsem.at[k],
            device_id=((ctx + PLANE * k) % (PLANE * NZ), y), device_id_type=MESH,
        )

    z_order = sorted(range(1, NZ), key=lambda k: -min(k, NZ - k))

    with jax.named_scope("loads"):
        own.wait()
        w_copy.wait()

    def project(part, slot, half):
        r = pl.ds(pl.multiple_of(half * half_rows, half_rows), half_rows)
        f = pl.ds(pl.multiple_of(slot * feat, feat), feat)
        return jnp.dot(tok_buf[slot, r, :], w_buf[part, f, :], preferred_element_type=F32)

    for part in range(3):
        f = pl.ds(pl.multiple_of(y * feat, feat), feat)
        acc[part] = jnp.dot(tok_buf[y], w_buf[part, f, :], preferred_element_type=F32)

    def token_step(i, carry):
        s, ci = i // 4 + 1, i % 4
        d, half = ci % 2, (ci + ci // 2) % 2
        slot = ring_take(tok_buf, tsend, trecv, d, half, s)

        @pl.when(jnp.logical_or(d == half, s < near))
        def _():
            ring_copy(tok_buf.at[slot], tok_buf, tsend, trecv, d, half, s, slot).start()

        r = pl.ds(pl.multiple_of(half * half_rows, half_rows), half_rows)
        for part in range(3):
            acc[part, r, :] = acc[part, r, :] + project(part, slot, half)

        @pl.when(y > 0)
        def _():
            @pl.when(jnp.logical_and(i == chain_at, z > 1))
            def _():
                chain_down()

            @pl.when(i == 3)
            def _():
                plane_heard(0)
                plane_hello(1)

            @pl.when(i == 5)
            def _():
                plane_heard(1)
                plane_hello(2)

            @pl.when(i == 7)
            def _():
                plane_heard(2)
                tell_first_row(0)

        @pl.when(i == 8)
        def _():
            first_row_heard(0)
            for q in range(1, PLANE):
                l_copy(q).start()
            lp_buf[j] = l_send[j // 4]

        return carry

    with jax.named_scope("token_ring"):
        lax.fori_loop(0, steps, token_step, 0)

    with jax.named_scope("token_last"):
        ring_take(tok_buf, tsend, trecv, 0, 0, far)
        slot = ring_take(tok_buf, tsend, trecv, 1, 1, far)
        f = pl.ds(pl.multiple_of(slot * feat, feat), feat)

        def finish(part):
            return (acc[part] + jnp.dot(tok_buf[slot], w_buf[part, f, :], preferred_element_type=F32)).astype(BF16)

    with jax.named_scope("local_state"):
        k_buf[...] = finish(1)
        v_buf[...] = finish(2)
        per = PLANE // HEADS
        seg = DH // per
        for h in range(HEADS):
            cols = slice(h * DH, (h + 1) * DH)
            weighted = (k_buf[:, cols].astype(F32) * keep_buf[h]).astype(BF16)
            local = lax.dot_general(weighted, v_buf[:, cols], (((0,), (0,)), ((), ())), preferred_element_type=F32)
            s_buf[h * per : (h + 1) * per] = local.astype(BF16).reshape(per, seg, DH)
        for q in range(1, PLANE):
            s_copy(q).start()
        sp_buf[j] = s_buf[j]

    with jax.named_scope("plane_logs"):
        @pl.when(jnp.logical_and(y > 0, z <= 1))
        def _():
            chain_down()

        tell_first_row(1)
        first_row_heard(1)
        for q in range(1, PLANE):
            l_copy(q).wait()
        total = lp_buf[0]
        for b in range(1, PLANE):
            total = total + lp_buf[b]
        lz_send[...] = total
        for k in z_order:
            @pl.when(z + k < NZ)
            def _():
                z_copy(lz_send, lz_recv, lzs, lzr, k).start()

    with jax.named_scope("intra"):
        query = finish(0)
        for h in range(HEADS):
            cols = slice(h * DH, (h + 1) * DH)
            scores = lax.dot_general(query[:, cols], k_buf[:, cols], (((1,), (1,)), ((), ())), preferred_element_type=F32)
            weights = (scores * dec_buf[h]).astype(BF16)
            intra_buf[h] = jnp.dot(weights, v_buf[:, cols], preferred_element_type=F32)

    with jax.named_scope("plane_totals"):
        for q in range(1, PLANE):
            s_copy(q).wait_recv()
        state = jnp.zeros((seg, DH), F32)
        gone = jnp.zeros((8, DH), F32)
        for b in range(PLANE):
            pre_buf[b] = state
            log_b = jnp.concatenate([lp_buf[b]] * (seg // 8), axis=0)
            state = jnp.exp(log_b) * state + sp_buf[b].astype(F32)
        t_send[...] = state.astype(BF16)
        for k in z_order:
            @pl.when(z + k < NZ)
            def _():
                z_copy(t_send, t_recv, tzs, tzr, k).start()

    with jax.named_scope("plane_weights"):
        run = jnp.zeros((8, DH), F32)
        for k in range(1, NZ):
            wz_buf[k] = jnp.exp(run)

            @pl.when(z >= k)
            def _():
                z_copy(lz_send, lz_recv, lzs, lzr, k).wait_recv()

            @pl.when(z < k)
            def _():
                lz_recv[k] = jnp.zeros((8, DH), F32)

            run = run + lz_recv[k]

    with jax.named_scope("earlier_planes"):
        pre_buf[PLANE] = jnp.zeros((seg, DH), F32)
        for k in range(1, NZ):
            @pl.when(z >= k)
            def _():
                z_copy(t_send, t_recv, tzs, tzr, k).wait_recv()
                w_k = jnp.concatenate([wz_buf[k]] * (seg // 8), axis=0)
                pre_buf[PLANE] = pre_buf[PLANE] + w_k * t_recv[k].astype(F32)

    with jax.named_scope("prefixes"):
        before = pre_buf[PLANE]
        for b in range(PLANE):
            gone_b = jnp.concatenate([jnp.exp(gone)] * (seg // 8), axis=0)
            st_send[b] = (gone_b * before + pre_buf[b]).astype(BF16)
            gone = gone + lp_buf[b]
        for q in range(1, PLANE):
            st_copy(q).start()
        st_recv[j] = st_send[j]
        for q in range(1, PLANE):
            st_copy(q).wait_recv()

    with jax.named_scope("normed"):
        for h in range(HEADS):
            cols = slice(h * DH, (h + 1) * DH)
            prev = st_recv[h * per : (h + 1) * per].reshape(DH, DH)
            inter = jnp.dot(query[:, cols], prev, preferred_element_type=F32) * eb_buf[h]
            attn = intra_buf[h] + inter
            normed = attn * lax.rsqrt(jnp.mean(attn * attn, axis=1, keepdims=True) + 1e-6)
            n_buf[y, :, cols] = normed.astype(BF16)

    ring_start(n_buf.at[y], n_buf, nsend, nrecv)
    width = HEADS * DH
    wout_copy.wait()
    f = pl.ds(pl.multiple_of(y * width, width), width)
    oacc[...] = jnp.dot(n_buf[y], wout_buf[f, :], preferred_element_type=F32)

    def out_step(i, carry):
        s, ci = i // 4 + 1, i % 4
        d, half = ci % 2, (ci + ci // 2) % 2
        slot = ring_take(n_buf, nsend, nrecv, d, half, s)

        @pl.when(jnp.logical_or(d == half, s < near))
        def _():
            ring_copy(n_buf.at[slot], n_buf, nsend, nrecv, d, half, s, slot).start()

        r = pl.ds(pl.multiple_of(half * half_rows, half_rows), half_rows)
        f = pl.ds(pl.multiple_of(slot * width, width), width)
        oacc[r, :] = oacc[r, :] + jnp.dot(n_buf[slot, r, :], wout_buf[f, :], preferred_element_type=F32)
        return carry

    with jax.named_scope("out_ring"):
        lax.fori_loop(0, steps, out_step, 0)
    with jax.named_scope("out_last"):
        ring_take(n_buf, nsend, nrecv, 0, 0, far)
        slot = ring_take(n_buf, nsend, nrecv, 1, 1, far)
        f = pl.ds(pl.multiple_of(slot * width, width), width)
        out_ref[...] = (oacc[...] + jnp.dot(n_buf[slot], wout_buf[f, :], preferred_element_type=F32)).astype(BF16)

    with jax.named_scope("drain"):
        ring_drain(tok_hbm, tok_buf, tsend, trecv)
        ring_drain(n_buf.at[y], n_buf, nsend, nrecv)
        for q in range(1, PLANE):
            s_copy(q).wait_send()
            st_copy(q).wait_send()
        for k in range(1, NZ):
            @pl.when(z + k < NZ)
            def _():
                z_copy(lz_send, lz_recv, lzs, lzr, k).wait_send()
                z_copy(t_send, t_recv, tzs, tzr, k).wait_send()


def body(NY, NZ, tokens, w_qkv, log_gate, w_out):
    rows, feat = tokens.shape
    width = HEADS * DH
    seg = HEADS * DH // PLANE
    dma = pltpu.SemaphoreType.DMA
    far = NY // 2
    any_spec = pl.BlockSpec(memory_space=pl.ANY)
    vmem_spec = pl.BlockSpec(memory_space=pltpu.VMEM)
    w3 = jnp.transpose(w_qkv, (1, 0, 2))
    gates = jnp.transpose(log_gate, (1, 0))
    scratch = [
        pltpu.VMEM((NY, rows, feat), BF16),
        pltpu.VMEM(w3.shape, BF16),
        pltpu.VMEM(w_out.shape, BF16),
        pltpu.VMEM((3, rows, width), F32),
        pltpu.VMEM((rows, width), BF16),
        pltpu.VMEM((rows, width), BF16),
        pltpu.VMEM((HEADS, rows, rows), F32),
        pltpu.VMEM((HEADS, rows, DH), F32),
        pltpu.VMEM((HEADS, rows, DH), F32),
        pltpu.VMEM((HEADS, rows, DH), F32),
        pltpu.VMEM((NY, rows, width), BF16),
        pltpu.VMEM((rows, w_out.shape[1]), F32),
        pltpu.VMEM((PLANE, seg, DH), BF16),
        pltpu.VMEM((PLANE, seg, DH), BF16),
        pltpu.VMEM((PLANE + 1, seg, DH), F32),
        pltpu.VMEM((seg, DH), BF16),
        pltpu.VMEM((NZ, seg, DH), BF16),
        pltpu.VMEM((PLANE, seg, DH), BF16),
        pltpu.VMEM((PLANE, seg, DH), BF16),
        pltpu.VMEM((HEADS, 8, DH), F32),
        pltpu.VMEM((PLANE, 8, DH), F32),
        pltpu.VMEM((8, DH), F32),
        pltpu.VMEM((NZ, 8, DH), F32),
        pltpu.VMEM((NZ, 8, DH), F32),
        dma, dma, dma,
        dma((2, 2, far)), dma((2, 2, far)), dma((2, 2, far)), dma((2, 2, far)),
        pltpu.SemaphoreType.REGULAR,
        pltpu.SemaphoreType.REGULAR,
        pltpu.SemaphoreType.REGULAR((3, 3)),
        pltpu.SemaphoreType.REGULAR((2,)),
        dma((PLANE,)), dma((PLANE,)),
        dma((NZ,)), dma((NZ,)),
        dma((PLANE,)), dma((PLANE,)),
        dma((NZ,)), dma((NZ,)),
        dma((PLANE,)), dma((PLANE,)),
    ]
    return pl.pallas_call(
        functools.partial(kernel, NY, NZ),
        out_shape=jax.ShapeDtypeStruct((rows, w_out.shape[1]), BF16),
        in_specs=[any_spec, any_spec, vmem_spec, any_spec],
        out_specs=vmem_spec,
        scratch_shapes=scratch,
        compiler_params=pltpu.CompilerParams(
            collective_id=0, has_side_effects=True, vmem_limit_bytes=63 << 20
        ),
    )(tokens, w3, gates, w_out)


def solution(mesh):
    placed = (P("ctx", "head"), P(None, None, "head"), P("ctx", "head"), P(None, "head"))
    return jax.shard_map(
        functools.partial(body, mesh.shape["head"], mesh.shape["ctx"] // PLANE),
        mesh=mesh, in_specs=placed, out_specs=P("ctx", "head"), check_vma=False,
    )
```

```python
import functools

import jax
import jax.numpy as jnp
from jax import lax
from jax.experimental import pallas as pl
from jax.experimental.pallas import tpu as pltpu
from jax.sharding import PartitionSpec as P

DH = 128
PLANE = 8
HEADS = 2
MESH = pl.DeviceIdType.MESH
F32 = jnp.float32
BF16 = jnp.bfloat16


def kernel(
    NY, NZ, tok_hbm, w_hbm, gate_ref, wout_hbm, out_ref,
    tok_buf, w_buf, wout_buf, acc, k_buf, v_buf, dec_buf, keep_buf, eb_buf, intra_buf,
    n_buf, oacc, s_buf, sp_buf, pre_buf, t_send, t_recv, st_send, st_recv,
    l_send, lp_buf, lz_send, lz_recv, wz_buf,
    w_sem, wout_sem, own_sem, tsend, trecv, nsend, nrecv,
    zh, ph, relay, lps, lpr, lzs, lzr, sps, spr, tzs, tzr, sts, strv,
):
    ctx = lax.axis_index("ctx")
    y = lax.axis_index("head")
    z, j = ctx // PLANE, ctx % PLANE
    x, core = j // 2, j % 2
    feat = tok_hbm.shape[1]
    rows = tok_hbm.shape[0]
    half_rows = rows // 2
    scale = DH ** (-0.5)

    right, left = (y + 1) % NY, (y + NY - 1) % NY
    jxr = ((x + 1) % 4) * 2 + core
    jxl = ((x + 3) % 4) * 2 + core
    jcore = x * 2 + (1 - core)
    zr = ((z + 1) % NZ) * PLANE + j
    zl = ((z + NZ - 1) % NZ) * PLANE + j
    base = z * PLANE

    own = pltpu.make_async_copy(tok_hbm, tok_buf.at[y], own_sem)
    own.start()
    w_copy = pltpu.make_async_copy(w_hbm, w_buf, w_sem)
    w_copy.start()
    wout_copy = pltpu.make_async_copy(wout_hbm, wout_buf, wout_sem)

    barrier = pltpu.get_barrier_semaphore()
    for dev in ((ctx, right), (ctx, left)):
        pl.semaphore_signal(barrier, inc=1, device_id=dev, device_id_type=MESH)

    @pl.when(y > 0)
    def _():
        for dev in (base + jxr, base + jxl, base + jcore, zl):
            pl.semaphore_signal(barrier, inc=1, device_id=(dev, y), device_id_type=MESH)

    with jax.named_scope("entry"):
        @pl.when(y > 0)
        def _():
            pl.semaphore_wait(barrier, 6)

        @pl.when(y == 0)
        def _():
            pl.semaphore_wait(barrier, 2)

    far = NY // 2
    near = NY - 1 - far

    def ring_copy(src, buf, ssem, rsem, d, half, s, slot):
        to = jnp.where(d == 0, right, left)
        part = pl.ds(pl.multiple_of(half * half_rows, half_rows), half_rows)
        return pltpu.make_async_remote_copy(
            src_ref=src.at[part], dst_ref=buf.at[slot, part],
            send_sem=ssem.at[d, half, s], recv_sem=rsem.at[d, half, s],
            device_id=(ctx, to), device_id_type=MESH,
        )

    def origin(d, s):
        return jnp.where(d == 0, y + NY - s, y + s) % NY

    def ring_start(src, buf, ssem, rsem):
        for d, half in ((0, 0), (1, 1), (0, 1), (1, 0)):
            if (d == half) or near > 0:
                ring_copy(src, buf, ssem, rsem, d, half, 0, y).start()

    def ring_take(buf, ssem, rsem, d, half, s):
        slot = origin(d, s)
        ring_copy(buf.at[slot], buf, ssem, rsem, d, half, s - 1, slot).wait_recv()
        return slot

    def ring_drain(src, buf, ssem, rsem):
        for d, half in ((0, 0), (1, 1), (0, 1), (1, 0)):
            for s in range(far if d == half else near):
                ring_copy(src, buf, ssem, rsem, d, half, s, y).wait_send()

    ring_start(tok_hbm, tok_buf, tsend, trecv)
    wout_copy.start()

    steps = 4 * near
    up_rounds, down_rounds = NZ // 2, NZ // 2 - 1
    up_from = jnp.maximum(0, jnp.minimum(4, 3 * NZ // 4 - z))
    down_from = 5

    def hello_up(r):
        pl.semaphore_signal(zh.at[0, r], inc=1, device_id=(zr, y), device_id_type=MESH)

    def hello_down(r):
        pl.semaphore_signal(zh.at[1, r], inc=1, device_id=(zl, y), device_id_type=MESH)

    def plane_hello(r):
        pl.semaphore_signal(ph.at[r, 0], inc=1, device_id=(base + jxr, y), device_id_type=MESH)
        pl.semaphore_signal(ph.at[r, 1], inc=1, device_id=(base + jxl, y), device_id_type=MESH)
        pl.semaphore_signal(ph.at[r, 2], inc=1, device_id=(base + jcore, y), device_id_type=MESH)

    def plane_heard(r):
        for q in range(3):
            pl.semaphore_wait(ph.at[r, q], 1)

    def tell_first_row(r):
        @pl.when(y == 1)
        def _():
            pl.semaphore_signal(relay.at[r], inc=1, device_id=(ctx, 0), device_id_type=MESH)

    def first_row_heard(r):
        @pl.when(y == 0)
        def _():
            pl.semaphore_wait(relay.at[r], 1)

    @pl.when(y > 0)
    def _():
        hello_up(0)
        plane_hello(0)

    with jax.named_scope("gates"):
        rid = lax.broadcasted_iota(jnp.int32, (rows, rows), 0)
        cid = lax.broadcasted_iota(jnp.int32, (rows, rows), 1)
        causal = cid <= rid
        for h in range(HEADS):
            g_row = gate_ref[h : h + 1, :]
            b_col = jnp.sum(jnp.where(causal, g_row, 0.0), axis=1, keepdims=True)
            b_row = jnp.sum(jnp.where(cid == rid, b_col, 0.0), axis=0, keepdims=True)
            last = b_col[rows - 1 : rows, :]
            diff = jnp.where(causal, b_col - b_row, 0.0)
            dec_buf[h] = jnp.where(causal, jnp.exp(diff) * scale, 0.0)
            keep_buf[h] = jnp.broadcast_to(jnp.exp(last - b_col), (rows, DH))
            eb_buf[h] = jnp.broadcast_to(jnp.exp(b_col) * scale, (rows, DH))
            l_send[h] = jnp.broadcast_to(last, (8, DH))

    def plane_copy(src, dst, ssem, rsem, d):
        to = (j + d) % PLANE
        return pltpu.make_async_remote_copy(
            src_ref=src(to), dst_ref=dst.at[j], send_sem=ssem.at[d], recv_sem=rsem.at[d],
            device_id=(base + to, y), device_id_type=MESH,
        )

    def l_copy(d):
        return plane_copy(lambda to: l_send.at[to // 4], lp_buf, lps, lpr, d)

    def s_copy(d):
        return plane_copy(lambda to: s_buf.at[to], sp_buf, sps, spr, d)

    def st_copy(d):
        return plane_copy(lambda to: st_send.at[to], st_recv, sts, strv, d)

    def z_copy(src, dst, ssem, rsem, k):
        return pltpu.make_async_remote_copy(
            src_ref=src, dst_ref=dst.at[k], send_sem=ssem.at[k], recv_sem=rsem.at[k],
            device_id=((ctx + PLANE * k) % (PLANE * NZ), y), device_id_type=MESH,
        )

    z_order = sorted(range(1, NZ), key=lambda k: -min(k, NZ - k))

    with jax.named_scope("loads"):
        own.wait()
        w_copy.wait()

    def project(part, slot, half):
        r = pl.ds(pl.multiple_of(half * half_rows, half_rows), half_rows)
        f = pl.ds(pl.multiple_of(slot * feat, feat), feat)
        return jnp.dot(tok_buf[slot, r, :], w_buf[part, f, :], preferred_element_type=F32)

    for part in range(3):
        f = pl.ds(pl.multiple_of(y * feat, feat), feat)
        acc[part] = jnp.dot(tok_buf[y], w_buf[part, f, :], preferred_element_type=F32)

    def token_step(i, carry):
        s, ci = i // 4 + 1, i % 4
        d, half = ci % 2, (ci + ci // 2) % 2
        slot = ring_take(tok_buf, tsend, trecv, d, half, s)

        @pl.when(jnp.logical_or(d == half, s < near))
        def _():
            ring_copy(tok_buf.at[slot], tok_buf, tsend, trecv, d, half, s, slot).start()

        r = pl.ds(pl.multiple_of(half * half_rows, half_rows), half_rows)
        for part in range(3):
            acc[part, r, :] = acc[part, r, :] + project(part, slot, half)

        @pl.when(y > 0)
        def _():
            up, down = i - up_from, i - down_from

            @pl.when(jnp.logical_and(up >= 0, up < up_rounds))
            def _():
                pl.semaphore_wait(zh.at[0, up], 1)

                @pl.when(up == 0)
                def _():
                    hello_down(0)

                @pl.when(up + 1 < up_rounds)
                def _():
                    hello_up(up + 1)

            @pl.when(jnp.logical_and(down >= 0, down < down_rounds))
            def _():
                pl.semaphore_wait(zh.at[1, down], 1)

                @pl.when(down + 1 < down_rounds)
                def _():
                    hello_down(down + 1)

            @pl.when(i == 3)
            def _():
                plane_heard(0)
                plane_hello(1)

            @pl.when(i == 5)
            def _():
                plane_heard(1)
                plane_hello(2)

            @pl.when(i == 7)
            def _():
                plane_heard(2)
                tell_first_row(0)

        @pl.when(i == 8)
        def _():
            first_row_heard(0)
            for q in range(1, PLANE):
                l_copy(q).start()
            lp_buf[j] = l_send[j // 4]

        return carry

    with jax.named_scope("token_ring"):
        lax.fori_loop(0, steps, token_step, 0)

    with jax.named_scope("token_last"):
        ring_take(tok_buf, tsend, trecv, 0, 0, far)
        slot = ring_take(tok_buf, tsend, trecv, 1, 1, far)
        f = pl.ds(pl.multiple_of(slot * feat, feat), feat)

        def finish(part):
            return (acc[part] + jnp.dot(tok_buf[slot], w_buf[part, f, :], preferred_element_type=F32)).astype(BF16)

    with jax.named_scope("local_state"):
        k_buf[...] = finish(1)
        v_buf[...] = finish(2)
        per = PLANE // HEADS
        seg = DH // per
        for h in range(HEADS):
            cols = slice(h * DH, (h + 1) * DH)
            weighted = (k_buf[:, cols].astype(F32) * keep_buf[h]).astype(BF16)
            local = lax.dot_general(weighted, v_buf[:, cols], (((0,), (0,)), ((), ())), preferred_element_type=F32)
            s_buf[h * per : (h + 1) * per] = local.astype(BF16).reshape(per, seg, DH)
        for q in range(1, PLANE):
            s_copy(q).start()
        sp_buf[j] = s_buf[j]

    with jax.named_scope("plane_logs"):
        tell_first_row(1)
        first_row_heard(1)
        for q in range(1, PLANE):
            l_copy(q).wait()
        total = lp_buf[0]
        for b in range(1, PLANE):
            total = total + lp_buf[b]
        lz_send[...] = total
        for k in z_order:
            @pl.when(z + k < NZ)
            def _():
                z_copy(lz_send, lz_recv, lzs, lzr, k).start()

    with jax.named_scope("intra"):
        query = finish(0)
        for h in range(HEADS):
            cols = slice(h * DH, (h + 1) * DH)
            scores = lax.dot_general(query[:, cols], k_buf[:, cols], (((1,), (1,)), ((), ())), preferred_element_type=F32)
            weights = (scores * dec_buf[h]).astype(BF16)
            intra_buf[h] = jnp.dot(weights, v_buf[:, cols], preferred_element_type=F32)

    with jax.named_scope("plane_totals"):
        for q in range(1, PLANE):
            s_copy(q).wait_recv()
        state = jnp.zeros((seg, DH), F32)
        gone = jnp.zeros((8, DH), F32)
        for b in range(PLANE):
            pre_buf[b] = state
            log_b = jnp.concatenate([lp_buf[b]] * (seg // 8), axis=0)
            state = jnp.exp(log_b) * state + sp_buf[b].astype(F32)
        t_send[...] = state.astype(BF16)
        for k in z_order:
            @pl.when(z + k < NZ)
            def _():
                z_copy(t_send, t_recv, tzs, tzr, k).start()

    with jax.named_scope("plane_weights"):
        run = jnp.zeros((8, DH), F32)
        for k in range(1, NZ):
            wz_buf[k] = jnp.exp(run)

            @pl.when(z >= k)
            def _():
                z_copy(lz_send, lz_recv, lzs, lzr, k).wait_recv()

            @pl.when(z < k)
            def _():
                lz_recv[k] = jnp.zeros((8, DH), F32)

            run = run + lz_recv[k]

    with jax.named_scope("earlier_planes"):
        pre_buf[PLANE] = jnp.zeros((seg, DH), F32)
        for k in range(1, NZ):
            @pl.when(z >= k)
            def _():
                z_copy(t_send, t_recv, tzs, tzr, k).wait_recv()
                w_k = jnp.concatenate([wz_buf[k]] * (seg // 8), axis=0)
                pre_buf[PLANE] = pre_buf[PLANE] + w_k * t_recv[k].astype(F32)

    with jax.named_scope("prefixes"):
        before = pre_buf[PLANE]
        for b in range(PLANE):
            gone_b = jnp.concatenate([jnp.exp(gone)] * (seg // 8), axis=0)
            st_send[b] = (gone_b * before + pre_buf[b]).astype(BF16)
            gone = gone + lp_buf[b]
        for q in range(1, PLANE):
            st_copy(q).start()
        st_recv[j] = st_send[j]
        for q in range(1, PLANE):
            st_copy(q).wait_recv()

    with jax.named_scope("normed"):
        for half in range(2):
            r = slice(half * half_rows, (half + 1) * half_rows)
            for h in range(HEADS):
                cols = slice(h * DH, (h + 1) * DH)
                prev = st_recv[h * per : (h + 1) * per].reshape(DH, DH)
                inter = jnp.dot(query[r, cols], prev, preferred_element_type=F32) * eb_buf[h, r, :]
                attn = intra_buf[h, r, :] + inter
                normed = attn * lax.rsqrt(jnp.mean(attn * attn, axis=1, keepdims=True) + 1e-6)
                n_buf[y, r, cols] = normed.astype(BF16)
            for d in (half, 1 - half):
                if d == half or near > 0:
                    ring_copy(n_buf.at[y], n_buf, nsend, nrecv, d, half, 0, y).start()

    width = HEADS * DH
    wout_copy.wait()
    f = pl.ds(pl.multiple_of(y * width, width), width)
    oacc[...] = jnp.dot(n_buf[y], wout_buf[f, :], preferred_element_type=F32)

    def out_step(i, carry):
        s, ci = i // 4 + 1, i % 4
        d, half = ci % 2, (ci + ci // 2) % 2
        slot = ring_take(n_buf, nsend, nrecv, d, half, s)

        @pl.when(jnp.logical_or(d == half, s < near))
        def _():
            ring_copy(n_buf.at[slot], n_buf, nsend, nrecv, d, half, s, slot).start()

        r = pl.ds(pl.multiple_of(half * half_rows, half_rows), half_rows)
        f = pl.ds(pl.multiple_of(slot * width, width), width)
        oacc[r, :] = oacc[r, :] + jnp.dot(n_buf[slot, r, :], wout_buf[f, :], preferred_element_type=F32)
        return carry

    with jax.named_scope("out_ring"):
        lax.fori_loop(0, steps, out_step, 0)
    with jax.named_scope("out_last"):
        ring_take(n_buf, nsend, nrecv, 0, 0, far)
        slot = ring_take(n_buf, nsend, nrecv, 1, 1, far)
        f = pl.ds(pl.multiple_of(slot * width, width), width)
        out_ref[...] = (oacc[...] + jnp.dot(n_buf[slot], wout_buf[f, :], preferred_element_type=F32)).astype(BF16)

    with jax.named_scope("drain"):
        ring_drain(tok_hbm, tok_buf, tsend, trecv)
        ring_drain(n_buf.at[y], n_buf, nsend, nrecv)
        for q in range(1, PLANE):
            s_copy(q).wait_send()
            st_copy(q).wait_send()
        for k in range(1, NZ):
            @pl.when(z + k < NZ)
            def _():
                z_copy(lz_send, lz_recv, lzs, lzr, k).wait_send()
                z_copy(t_send, t_recv, tzs, tzr, k).wait_send()


def body(NY, NZ, tokens, w_qkv, log_gate, w_out):
    rows, feat = tokens.shape
    width = HEADS * DH
    seg = HEADS * DH // PLANE
    dma = pltpu.SemaphoreType.DMA
    far = NY // 2
    any_spec = pl.BlockSpec(memory_space=pl.ANY)
    vmem_spec = pl.BlockSpec(memory_space=pltpu.VMEM)
    w3 = jnp.transpose(w_qkv, (1, 0, 2))
    gates = jnp.transpose(log_gate, (1, 0))
    scratch = [
        pltpu.VMEM((NY, rows, feat), BF16),
        pltpu.VMEM(w3.shape, BF16),
        pltpu.VMEM(w_out.shape, BF16),
        pltpu.VMEM((3, rows, width), F32),
        pltpu.VMEM((rows, width), BF16),
        pltpu.VMEM((rows, width), BF16),
        pltpu.VMEM((HEADS, rows, rows), F32),
        pltpu.VMEM((HEADS, rows, DH), F32),
        pltpu.VMEM((HEADS, rows, DH), F32),
        pltpu.VMEM((HEADS, rows, DH), F32),
        pltpu.VMEM((NY, rows, width), BF16),
        pltpu.VMEM((rows, w_out.shape[1]), F32),
        pltpu.VMEM((PLANE, seg, DH), BF16),
        pltpu.VMEM((PLANE, seg, DH), BF16),
        pltpu.VMEM((PLANE + 1, seg, DH), F32),
        pltpu.VMEM((seg, DH), BF16),
        pltpu.VMEM((NZ, seg, DH), BF16),
        pltpu.VMEM((PLANE, seg, DH), BF16),
        pltpu.VMEM((PLANE, seg, DH), BF16),
        pltpu.VMEM((HEADS, 8, DH), F32),
        pltpu.VMEM((PLANE, 8, DH), F32),
        pltpu.VMEM((8, DH), F32),
        pltpu.VMEM((NZ, 8, DH), F32),
        pltpu.VMEM((NZ, 8, DH), F32),
        dma, dma, dma,
        dma((2, 2, far)), dma((2, 2, far)), dma((2, 2, far)), dma((2, 2, far)),
        pltpu.SemaphoreType.REGULAR((2, NZ // 2)),
        pltpu.SemaphoreType.REGULAR((3, 3)),
        pltpu.SemaphoreType.REGULAR((2,)),
        dma((PLANE,)), dma((PLANE,)),
        dma((NZ,)), dma((NZ,)),
        dma((PLANE,)), dma((PLANE,)),
        dma((NZ,)), dma((NZ,)),
        dma((PLANE,)), dma((PLANE,)),
    ]
    return pl.pallas_call(
        functools.partial(kernel, NY, NZ),
        out_shape=jax.ShapeDtypeStruct((rows, w_out.shape[1]), BF16),
        in_specs=[any_spec, any_spec, vmem_spec, any_spec],
        out_specs=vmem_spec,
        scratch_shapes=scratch,
        compiler_params=pltpu.CompilerParams(
            collective_id=0, has_side_effects=True, vmem_limit_bytes=63 << 20
        ),
    )(tokens, w3, gates, w_out)


def solution(mesh):
    placed = (P("ctx", "head"), P(None, None, "head"), P("ctx", "head"), P(None, "head"))
    return jax.shard_map(
        functools.partial(body, mesh.shape["head"], mesh.shape["ctx"] // PLANE),
        mesh=mesh, in_specs=placed, out_specs=P("ctx", "head"), check_vma=False,
    )
```

```python
import functools

import jax
import jax.numpy as jnp
from jax import lax
from jax.experimental import pallas as pl
from jax.experimental.pallas import tpu as pltpu
from jax.sharding import PartitionSpec as P

DH = 128
PLANE = 8
HEADS = 2
MESH = pl.DeviceIdType.MESH
F32 = jnp.float32
BF16 = jnp.bfloat16


def kernel(
    NY, NZ, tok_hbm, w_hbm, gate_ref, wout_hbm, out_ref,
    tok_buf, w_buf, wout_buf, acc, k_buf, v_buf, dec_buf, keep_buf, eb_buf, intra_buf,
    n_buf, oacc, s_buf, sp_buf, pre_buf, t_send, t_recv, st_send, st_recv,
    l_send, lp_buf, lz_send, lz_recv, wz_buf,
    w_sem, wout_sem, own_sem, tsend, trecv, nsend, nrecv,
    zh, ph, relay, lps, lpr, lzs, lzr, sps, spr, tzs, tzr, sts, strv,
):
    ctx = lax.axis_index("ctx")
    y = lax.axis_index("head")
    z, j = ctx // PLANE, ctx % PLANE
    x, core = j // 2, j % 2
    feat = tok_hbm.shape[1]
    rows = tok_hbm.shape[0]
    half_rows = rows // 2
    scale = DH ** (-0.5)

    right, left = (y + 1) % NY, (y + NY - 1) % NY
    jxr = ((x + 1) % 4) * 2 + core
    jxl = ((x + 3) % 4) * 2 + core
    jcore = x * 2 + (1 - core)
    zr = ((z + 1) % NZ) * PLANE + j
    zl = ((z + NZ - 1) % NZ) * PLANE + j
    base = z * PLANE

    own = pltpu.make_async_copy(tok_hbm, tok_buf.at[y], own_sem)
    own.start()
    w_copy = pltpu.make_async_copy(w_hbm, w_buf, w_sem)
    w_copy.start()
    wout_copy = pltpu.make_async_copy(wout_hbm, wout_buf, wout_sem)

    barrier = pltpu.get_barrier_semaphore()
    for dev in ((ctx, right), (ctx, left)):
        pl.semaphore_signal(barrier, inc=1, device_id=dev, device_id_type=MESH)

    @pl.when(y > 0)
    def _():
        for dev in (base + jxr, base + jxl, base + jcore, zl):
            pl.semaphore_signal(barrier, inc=1, device_id=(dev, y), device_id_type=MESH)

    with jax.named_scope("entry"):
        @pl.when(y > 0)
        def _():
            pl.semaphore_wait(barrier, 6)

        @pl.when(y == 0)
        def _():
            pl.semaphore_wait(barrier, 2)

    far = NY // 2
    near = NY - 1 - far

    def ring_copy(src, buf, ssem, rsem, d, half, s, slot):
        to = jnp.where(d == 0, right, left)
        part = pl.ds(pl.multiple_of(half * half_rows, half_rows), half_rows)
        return pltpu.make_async_remote_copy(
            src_ref=src.at[part], dst_ref=buf.at[slot, part],
            send_sem=ssem.at[d, half, s], recv_sem=rsem.at[d, half, s],
            device_id=(ctx, to), device_id_type=MESH,
        )

    def origin(d, s):
        return jnp.where(d == 0, y + NY - s, y + s) % NY

    def ring_start(src, buf, ssem, rsem):
        for d, half in ((0, 0), (1, 1), (0, 1), (1, 0)):
            if (d == half) or near > 0:
                ring_copy(src, buf, ssem, rsem, d, half, 0, y).start()

    def ring_take(buf, ssem, rsem, d, half, s):
        slot = origin(d, s)
        ring_copy(buf.at[slot], buf, ssem, rsem, d, half, s - 1, slot).wait_recv()
        return slot

    def ring_drain(src, buf, ssem, rsem):
        for d, half in ((0, 0), (1, 1), (0, 1), (1, 0)):
            for s in range(far if d == half else near):
                ring_copy(src, buf, ssem, rsem, d, half, s, y).wait_send()

    ring_start(tok_hbm, tok_buf, tsend, trecv)
    wout_copy.start()

    steps = 4 * near
    up_rounds, down_rounds = NZ // 2, NZ // 2 - 1
    up_from = jnp.maximum(0, jnp.minimum(4, 3 * NZ // 4 - z))
    down_from = jnp.maximum(1, jnp.minimum(5, NZ // 2 + 1 - z))
    contact_at = jnp.where(z >= 2, 0, 4)

    def hello_up(r):
        pl.semaphore_signal(zh.at[0, r], inc=1, device_id=(zr, y), device_id_type=MESH)

    def hello_down(r):
        pl.semaphore_signal(zh.at[1, r], inc=1, device_id=(zl, y), device_id_type=MESH)

    def plane_hello(r):
        pl.semaphore_signal(ph.at[r, 0], inc=1, device_id=(base + jxr, y), device_id_type=MESH)
        pl.semaphore_signal(ph.at[r, 1], inc=1, device_id=(base + jxl, y), device_id_type=MESH)
        pl.semaphore_signal(ph.at[r, 2], inc=1, device_id=(base + jcore, y), device_id_type=MESH)

    def plane_heard(r):
        for q in range(3):
            pl.semaphore_wait(ph.at[r, q], 1)

    def tell_first_row(r):
        @pl.when(y == 1)
        def _():
            pl.semaphore_signal(relay.at[r], inc=1, device_id=(ctx, 0), device_id_type=MESH)

    def first_row_heard(r):
        @pl.when(y == 0)
        def _():
            pl.semaphore_wait(relay.at[r], 1)

    @pl.when(y > 0)
    def _():
        hello_up(0)
        plane_hello(0)

    with jax.named_scope("gates"):
        rid = lax.broadcasted_iota(jnp.int32, (rows, rows), 0)
        cid = lax.broadcasted_iota(jnp.int32, (rows, rows), 1)
        causal = cid <= rid
        for h in range(HEADS):
            g_row = gate_ref[h : h + 1, :]
            b_col = jnp.sum(jnp.where(causal, g_row, 0.0), axis=1, keepdims=True)
            b_row = jnp.sum(jnp.where(cid == rid, b_col, 0.0), axis=0, keepdims=True)
            last = b_col[rows - 1 : rows, :]
            diff = jnp.where(causal, b_col - b_row, 0.0)
            dec_buf[h] = jnp.where(causal, jnp.exp(diff) * scale, 0.0)
            keep_buf[h] = jnp.broadcast_to(jnp.exp(last - b_col), (rows, DH))
            eb_buf[h] = jnp.broadcast_to(jnp.exp(b_col) * scale, (rows, DH))
            l_send[h] = jnp.broadcast_to(last, (8, DH))

    def plane_copy(src, dst, ssem, rsem, d):
        to = (j + d) % PLANE
        return pltpu.make_async_remote_copy(
            src_ref=src(to), dst_ref=dst.at[j], send_sem=ssem.at[d], recv_sem=rsem.at[d],
            device_id=(base + to, y), device_id_type=MESH,
        )

    def l_copy(d):
        return plane_copy(lambda to: l_send.at[to // 4], lp_buf, lps, lpr, d)

    def s_copy(d):
        return plane_copy(lambda to: s_buf.at[to], sp_buf, sps, spr, d)

    def st_copy(d):
        return plane_copy(lambda to: st_send.at[to], st_recv, sts, strv, d)

    def z_copy(src, dst, ssem, rsem, k):
        return pltpu.make_async_remote_copy(
            src_ref=src, dst_ref=dst.at[k], send_sem=ssem.at[k], recv_sem=rsem.at[k],
            device_id=((ctx + PLANE * k) % (PLANE * NZ), y), device_id_type=MESH,
        )

    z_order = sorted(range(1, NZ), key=lambda k: -min(k, NZ - k))

    with jax.named_scope("loads"):
        own.wait()
        w_copy.wait()

    def project(part, slot, half):
        r = pl.ds(pl.multiple_of(half * half_rows, half_rows), half_rows)
        f = pl.ds(pl.multiple_of(slot * feat, feat), feat)
        return jnp.dot(tok_buf[slot, r, :], w_buf[part, f, :], preferred_element_type=F32)

    for part in range(3):
        f = pl.ds(pl.multiple_of(y * feat, feat), feat)
        acc[part] = jnp.dot(tok_buf[y], w_buf[part, f, :], preferred_element_type=F32)

    def token_step(i, carry):
        s, ci = i // 4 + 1, i % 4
        d, half = ci % 2, (ci + ci // 2) % 2
        slot = ring_take(tok_buf, tsend, trecv, d, half, s)

        @pl.when(jnp.logical_or(d == half, s < near))
        def _():
            ring_copy(tok_buf.at[slot], tok_buf, tsend, trecv, d, half, s, slot).start()

        r = pl.ds(pl.multiple_of(half * half_rows, half_rows), half_rows)
        for part in range(3):
            acc[part, r, :] = acc[part, r, :] + project(part, slot, half)

        @pl.when(y > 0)
        def _():
            up, down = i - up_from, i - down_from
            wrapped = (z + 2 * NZ - 1 - up) % NZ >= NZ // 2

            @pl.when(i == contact_at)
            def _():
                pl.semaphore_wait(zh.at[0, 0], 1)

                @pl.when(z > 0)
                def _():
                    hello_down(0)

                @pl.when(jnp.logical_or(z == 0, z > NZ // 2))
                def _():
                    hello_up(1)

            @pl.when(jnp.logical_and(jnp.logical_and(down >= 0, down < down_rounds), z + 1 + down < NZ))
            def _():
                pl.semaphore_wait(zh.at[1, down], 1)

                @pl.when(jnp.logical_and(down + 1 < down_rounds, z > 0))
                def _():
                    hello_down(down + 1)

            @pl.when(jnp.logical_and(jnp.logical_and(up >= 1, up < up_rounds), wrapped))
            def _():
                pl.semaphore_wait(zh.at[0, up], 1)

                @pl.when(up + 1 < up_rounds)
                def _():
                    hello_up(up + 1)

            @pl.when(i == 3)
            def _():
                plane_heard(0)
                plane_hello(1)

            @pl.when(i == 5)
            def _():
                plane_heard(1)
                plane_hello(2)

            @pl.when(i == 7)
            def _():
                plane_heard(2)
                tell_first_row(0)

        return carry

    with jax.named_scope("token_ring"):
        lax.fori_loop(0, steps, token_step, 0)

    with jax.named_scope("token_last"):
        ring_take(tok_buf, tsend, trecv, 0, 0, far)
        slot = ring_take(tok_buf, tsend, trecv, 1, 1, far)
        f = pl.ds(pl.multiple_of(slot * feat, feat), feat)

        def finish(part):
            return (acc[part] + jnp.dot(tok_buf[slot], w_buf[part, f, :], preferred_element_type=F32)).astype(BF16)

    with jax.named_scope("local_state"):
        first_row_heard(0)
        for q in range(1, PLANE):
            l_copy(q).start()
        lp_buf[j] = l_send[j // 4]
        k_buf[...] = finish(1)
        v_buf[...] = finish(2)
        per = PLANE // HEADS
        seg = DH // per
        for h in range(HEADS):
            cols = slice(h * DH, (h + 1) * DH)
            weighted = (k_buf[:, cols].astype(F32) * keep_buf[h]).astype(BF16)
            local = lax.dot_general(weighted, v_buf[:, cols], (((0,), (0,)), ((), ())), preferred_element_type=F32)
            s_buf[h * per : (h + 1) * per] = local.astype(BF16).reshape(per, seg, DH)
        for q in range(1, PLANE):
            s_copy(q).start()
        sp_buf[j] = s_buf[j]

    with jax.named_scope("plane_logs"):
        tell_first_row(1)
        first_row_heard(1)
        for q in range(1, PLANE):
            l_copy(q).wait()
        total = lp_buf[0]
        for b in range(1, PLANE):
            total = total + lp_buf[b]
        lz_send[...] = total
        for k in z_order:
            @pl.when(z + k < NZ)
            def _():
                z_copy(lz_send, lz_recv, lzs, lzr, k).start()

    with jax.named_scope("intra"):
        query = finish(0)
        for h in range(HEADS):
            cols = slice(h * DH, (h + 1) * DH)
            scores = lax.dot_general(query[:, cols], k_buf[:, cols], (((1,), (1,)), ((), ())), preferred_element_type=F32)
            weights = (scores * dec_buf[h]).astype(BF16)
            intra_buf[h] = jnp.dot(weights, v_buf[:, cols], preferred_element_type=F32)

    with jax.named_scope("plane_totals"):
        for q in range(1, PLANE):
            s_copy(q).wait_recv()
        state = jnp.zeros((seg, DH), F32)
        gone = jnp.zeros((8, DH), F32)
        for b in range(PLANE):
            pre_buf[b] = state
            log_b = jnp.concatenate([lp_buf[b]] * (seg // 8), axis=0)
            state = jnp.exp(log_b) * state + sp_buf[b].astype(F32)
        t_send[...] = state.astype(BF16)
        for k in z_order:
            @pl.when(z + k < NZ)
            def _():
                z_copy(t_send, t_recv, tzs, tzr, k).start()

    with jax.named_scope("plane_weights"):
        run = jnp.zeros((8, DH), F32)
        for k in range(1, NZ):
            wz_buf[k] = jnp.exp(run)

            @pl.when(z >= k)
            def _():
                z_copy(lz_send, lz_recv, lzs, lzr, k).wait_recv()

            @pl.when(z < k)
            def _():
                lz_recv[k] = jnp.zeros((8, DH), F32)

            run = run + lz_recv[k]

    with jax.named_scope("earlier_planes"):
        pre_buf[PLANE] = jnp.zeros((seg, DH), F32)
        for k in range(1, NZ):
            @pl.when(z >= k)
            def _():
                z_copy(t_send, t_recv, tzs, tzr, k).wait_recv()
                w_k = jnp.concatenate([wz_buf[k]] * (seg // 8), axis=0)
                pre_buf[PLANE] = pre_buf[PLANE] + w_k * t_recv[k].astype(F32)

    with jax.named_scope("prefixes"):
        before = pre_buf[PLANE]
        for b in range(PLANE):
            gone_b = jnp.concatenate([jnp.exp(gone)] * (seg // 8), axis=0)
            st_send[b] = (gone_b * before + pre_buf[b]).astype(BF16)
            gone = gone + lp_buf[b]
        for q in range(1, PLANE):
            st_copy(q).start()
        st_recv[j] = st_send[j]
        for q in range(1, PLANE):
            st_copy(q).wait_recv()

    with jax.named_scope("normed"):
        for half in range(2):
            r = slice(half * half_rows, (half + 1) * half_rows)
            for h in range(HEADS):
                cols = slice(h * DH, (h + 1) * DH)
                prev = st_recv[h * per : (h + 1) * per].reshape(DH, DH)
                inter = jnp.dot(query[r, cols], prev, preferred_element_type=F32) * eb_buf[h, r, :]
                attn = intra_buf[h, r, :] + inter
                normed = attn * lax.rsqrt(jnp.mean(attn * attn, axis=1, keepdims=True) + 1e-6)
                n_buf[y, r, cols] = normed.astype(BF16)
            for d in (half, 1 - half):
                if d == half or near > 0:
                    ring_copy(n_buf.at[y], n_buf, nsend, nrecv, d, half, 0, y).start()

    width = HEADS * DH
    wout_copy.wait()
    f = pl.ds(pl.multiple_of(y * width, width), width)
    oacc[...] = jnp.dot(n_buf[y], wout_buf[f, :], preferred_element_type=F32)

    def out_step(i, carry):
        s, ci = i // 4 + 1, i % 4
        d, half = ci % 2, (ci + ci // 2) % 2
        slot = ring_take(n_buf, nsend, nrecv, d, half, s)

        @pl.when(jnp.logical_or(d == half, s < near))
        def _():
            ring_copy(n_buf.at[slot], n_buf, nsend, nrecv, d, half, s, slot).start()

        r = pl.ds(pl.multiple_of(half * half_rows, half_rows), half_rows)
        f = pl.ds(pl.multiple_of(slot * width, width), width)
        oacc[r, :] = oacc[r, :] + jnp.dot(n_buf[slot, r, :], wout_buf[f, :], preferred_element_type=F32)
        return carry

    with jax.named_scope("out_ring"):
        lax.fori_loop(0, steps, out_step, 0)
    with jax.named_scope("out_last"):
        ring_take(n_buf, nsend, nrecv, 0, 0, far)
        slot = ring_take(n_buf, nsend, nrecv, 1, 1, far)
        f = pl.ds(pl.multiple_of(slot * width, width), width)
        out_ref[...] = (oacc[...] + jnp.dot(n_buf[slot], wout_buf[f, :], preferred_element_type=F32)).astype(BF16)

    with jax.named_scope("drain"):
        ring_drain(tok_hbm, tok_buf, tsend, trecv)
        ring_drain(n_buf.at[y], n_buf, nsend, nrecv)
        for q in range(1, PLANE):
            s_copy(q).wait_send()
            st_copy(q).wait_send()
        for k in range(1, NZ):
            @pl.when(z + k < NZ)
            def _():
                z_copy(lz_send, lz_recv, lzs, lzr, k).wait_send()
                z_copy(t_send, t_recv, tzs, tzr, k).wait_send()


def body(NY, NZ, tokens, w_qkv, log_gate, w_out):
    rows, feat = tokens.shape
    width = HEADS * DH
    seg = HEADS * DH // PLANE
    dma = pltpu.SemaphoreType.DMA
    far = NY // 2
    any_spec = pl.BlockSpec(memory_space=pl.ANY)
    vmem_spec = pl.BlockSpec(memory_space=pltpu.VMEM)
    w3 = jnp.transpose(w_qkv, (1, 0, 2))
    gates = jnp.transpose(log_gate, (1, 0))
    scratch = [
        pltpu.VMEM((NY, rows, feat), BF16),
        pltpu.VMEM(w3.shape, BF16),
        pltpu.VMEM(w_out.shape, BF16),
        pltpu.VMEM((3, rows, width), F32),
        pltpu.VMEM((rows, width), BF16),
        pltpu.VMEM((rows, width), BF16),
        pltpu.VMEM((HEADS, rows, rows), F32),
        pltpu.VMEM((HEADS, rows, DH), F32),
        pltpu.VMEM((HEADS, rows, DH), F32),
        pltpu.VMEM((HEADS, rows, DH), F32),
        pltpu.VMEM((NY, rows, width), BF16),
        pltpu.VMEM((rows, w_out.shape[1]), F32),
        pltpu.VMEM((PLANE, seg, DH), BF16),
        pltpu.VMEM((PLANE, seg, DH), BF16),
        pltpu.VMEM((PLANE + 1, seg, DH), F32),
        pltpu.VMEM((seg, DH), BF16),
        pltpu.VMEM((NZ, seg, DH), BF16),
        pltpu.VMEM((PLANE, seg, DH), BF16),
        pltpu.VMEM((PLANE, seg, DH), BF16),
        pltpu.VMEM((HEADS, 8, DH), F32),
        pltpu.VMEM((PLANE, 8, DH), F32),
        pltpu.VMEM((8, DH), F32),
        pltpu.VMEM((NZ, 8, DH), F32),
        pltpu.VMEM((NZ, 8, DH), F32),
        dma, dma, dma,
        dma((2, 2, far)), dma((2, 2, far)), dma((2, 2, far)), dma((2, 2, far)),
        pltpu.SemaphoreType.REGULAR((2, NZ // 2)),
        pltpu.SemaphoreType.REGULAR((3, 3)),
        pltpu.SemaphoreType.REGULAR((2,)),
        dma((PLANE,)), dma((PLANE,)),
        dma((NZ,)), dma((NZ,)),
        dma((PLANE,)), dma((PLANE,)),
        dma((NZ,)), dma((NZ,)),
        dma((PLANE,)), dma((PLANE,)),
    ]
    return pl.pallas_call(
        functools.partial(kernel, NY, NZ),
        out_shape=jax.ShapeDtypeStruct((rows, w_out.shape[1]), BF16),
        in_specs=[any_spec, any_spec, vmem_spec, any_spec],
        out_specs=vmem_spec,
        scratch_shapes=scratch,
        compiler_params=pltpu.CompilerParams(
            collective_id=0, has_side_effects=True, vmem_limit_bytes=63 << 20
        ),
    )(tokens, w3, gates, w_out)


def solution(mesh):
    placed = (P("ctx", "head"), P(None, None, "head"), P("ctx", "head"), P(None, "head"))
    return jax.shard_map(
        functools.partial(body, mesh.shape["head"], mesh.shape["ctx"] // PLANE),
        mesh=mesh, in_specs=placed, out_specs=P("ctx", "head"), check_vma=False,
    )
```

```python
import functools

import jax
import jax.numpy as jnp
from jax import lax
from jax.experimental import pallas as pl
from jax.experimental.pallas import tpu as pltpu
from jax.sharding import PartitionSpec as P

DH = 128
PLANE = 8
HEADS = 2
MESH = pl.DeviceIdType.MESH
F32 = jnp.float32
BF16 = jnp.bfloat16


def kernel(
    NY, NZ, tok_hbm, w_hbm, gate_ref, wout_hbm, out_ref,
    tok_buf, w_buf, wout_buf, acc, k_buf, v_buf, dec_buf, keep_buf, eb_buf, intra_buf,
    n_buf, oacc, s_buf, sp_buf, pre_buf, t_send, t_recv, st_send, st_recv,
    l_send, lp_buf, lz_send, lz_recv, wz_buf,
    w_sem, wout_sem, own_sem, tsend, trecv, nsend, nrecv,
    zh, ph, relay, lps, lpr, lzs, lzr, sps, spr, tzs, tzr, sts, strv,
):
    ctx = lax.axis_index("ctx")
    y = lax.axis_index("head")
    z, j = ctx // PLANE, ctx % PLANE
    x, core = j // 2, j % 2
    feat = tok_hbm.shape[1]
    rows = tok_hbm.shape[0]
    half_rows = rows // 2
    scale = DH ** (-0.5)

    right, left = (y + 1) % NY, (y + NY - 1) % NY
    jxr = ((x + 1) % 4) * 2 + core
    jxl = ((x + 3) % 4) * 2 + core
    jcore = x * 2 + (1 - core)
    zr = ((z + 1) % NZ) * PLANE + j
    zl = ((z + NZ - 1) % NZ) * PLANE + j
    base = z * PLANE

    own = pltpu.make_async_copy(tok_hbm, tok_buf.at[y], own_sem)
    own.start()
    w_copy = pltpu.make_async_copy(w_hbm, w_buf, w_sem)
    w_copy.start()
    wout_copy = pltpu.make_async_copy(wout_hbm, wout_buf, wout_sem)

    barrier = pltpu.get_barrier_semaphore()
    for dev in ((ctx, right), (ctx, left)):
        pl.semaphore_signal(barrier, inc=1, device_id=dev, device_id_type=MESH)

    @pl.when(y > 0)
    def _():
        for dev in (base + jxr, base + jxl, base + jcore, zl):
            pl.semaphore_signal(barrier, inc=1, device_id=(dev, y), device_id_type=MESH)

    with jax.named_scope("entry"):
        @pl.when(y > 0)
        def _():
            pl.semaphore_wait(barrier, 6)

        @pl.when(y == 0)
        def _():
            pl.semaphore_wait(barrier, 2)

    far = NY // 2
    near = NY - 1 - far
    piece = half_rows // 2

    def ring_copy(src, buf, ssem, rsem, d, half, s, slot, q):
        to = jnp.where(d == 0, right, left)
        part = pl.ds(pl.multiple_of(half * half_rows + q * piece, piece), piece)
        return pltpu.make_async_remote_copy(
            src_ref=src.at[part], dst_ref=buf.at[slot, part],
            send_sem=ssem.at[d, half, s, q], recv_sem=rsem.at[d, half, s, q],
            device_id=(ctx, to), device_id_type=MESH,
        )

    def origin(d, s):
        return jnp.where(d == 0, y + NY - s, y + s) % NY

    def ring_start(src, buf, ssem, rsem):
        for d, half in ((0, 0), (1, 1), (0, 1), (1, 0)):
            if (d == half) or near > 0:
                for q in range(2):
                    ring_copy(src, buf, ssem, rsem, d, half, 0, y, q).start()

    def ring_take(buf, ssem, rsem, d, half, s, more):
        slot = origin(d, s)
        for q in range(2):
            ring_copy(buf.at[slot], buf, ssem, rsem, d, half, s - 1, slot, q).wait_recv()
            if more is not None:
                @pl.when(more)
                def _():
                    ring_copy(buf.at[slot], buf, ssem, rsem, d, half, s, slot, q).start()
        return slot

    def ring_drain(src, buf, ssem, rsem):
        for d, half in ((0, 0), (1, 1), (0, 1), (1, 0)):
            for s in range(far if d == half else near):
                for q in range(2):
                    ring_copy(src, buf, ssem, rsem, d, half, s, y, q).wait_send()

    ring_start(tok_hbm, tok_buf, tsend, trecv)
    wout_copy.start()

    steps = 4 * near
    up_rounds, down_rounds = NZ // 2, NZ // 2 - 1
    up_from = jnp.maximum(0, jnp.minimum(4, 3 * NZ // 4 - z))
    down_from = jnp.maximum(1, jnp.minimum(5, NZ // 2 + 1 - z))
    contact_at = jnp.where(z >= 2, 0, 4)

    def hello_up(r):
        pl.semaphore_signal(zh.at[0, r], inc=1, device_id=(zr, y), device_id_type=MESH)

    def hello_down(r):
        pl.semaphore_signal(zh.at[1, r], inc=1, device_id=(zl, y), device_id_type=MESH)

    def plane_hello(r):
        pl.semaphore_signal(ph.at[r, 0], inc=1, device_id=(base + jxr, y), device_id_type=MESH)
        pl.semaphore_signal(ph.at[r, 1], inc=1, device_id=(base + jxl, y), device_id_type=MESH)
        pl.semaphore_signal(ph.at[r, 2], inc=1, device_id=(base + jcore, y), device_id_type=MESH)

    def plane_heard(r):
        for q in range(3):
            pl.semaphore_wait(ph.at[r, q], 1)

    def tell_first_row(r):
        @pl.when(y == 1)
        def _():
            pl.semaphore_signal(relay.at[r], inc=1, device_id=(ctx, 0), device_id_type=MESH)

    def first_row_heard(r):
        @pl.when(y == 0)
        def _():
            pl.semaphore_wait(relay.at[r], 1)

    @pl.when(y > 0)
    def _():
        hello_up(0)
        plane_hello(0)

    with jax.named_scope("gates"):
        rid = lax.broadcasted_iota(jnp.int32, (rows, rows), 0)
        cid = lax.broadcasted_iota(jnp.int32, (rows, rows), 1)
        causal = cid <= rid
        for h in range(HEADS):
            g_row = gate_ref[h : h + 1, :]
            b_col = jnp.sum(jnp.where(causal, g_row, 0.0), axis=1, keepdims=True)
            b_row = jnp.sum(jnp.where(cid == rid, b_col, 0.0), axis=0, keepdims=True)
            last = b_col[rows - 1 : rows, :]
            diff = jnp.where(causal, b_col - b_row, 0.0)
            dec_buf[h] = jnp.where(causal, jnp.exp(diff) * scale, 0.0)
            keep_buf[h] = jnp.broadcast_to(jnp.exp(last - b_col), (rows, DH))
            eb_buf[h] = jnp.broadcast_to(jnp.exp(b_col) * scale, (rows, DH))
            l_send[h] = jnp.broadcast_to(last, (8, DH))

    def plane_copy(src, dst, ssem, rsem, d):
        to = (j + d) % PLANE
        return pltpu.make_async_remote_copy(
            src_ref=src(to), dst_ref=dst.at[j], send_sem=ssem.at[d], recv_sem=rsem.at[d],
            device_id=(base + to, y), device_id_type=MESH,
        )

    def l_copy(d):
        return plane_copy(lambda to: l_send.at[to // 4], lp_buf, lps, lpr, d)

    def s_copy(d):
        return plane_copy(lambda to: s_buf.at[to], sp_buf, sps, spr, d)

    def st_copy(d):
        return plane_copy(lambda to: st_send.at[to], st_recv, sts, strv, d)

    def z_copy(src, dst, ssem, rsem, k):
        return pltpu.make_async_remote_copy(
            src_ref=src, dst_ref=dst.at[k], send_sem=ssem.at[k], recv_sem=rsem.at[k],
            device_id=((ctx + PLANE * k) % (PLANE * NZ), y), device_id_type=MESH,
        )

    z_order = sorted(range(1, NZ), key=lambda k: -min(k, NZ - k))

    with jax.named_scope("loads"):
        own.wait()
        w_copy.wait()

    def project(part, slot, half):
        r = pl.ds(pl.multiple_of(half * half_rows, half_rows), half_rows)
        f = pl.ds(pl.multiple_of(slot * feat, feat), feat)
        return jnp.dot(tok_buf[slot, r, :], w_buf[part, f, :], preferred_element_type=F32)

    for part in range(3):
        f = pl.ds(pl.multiple_of(y * feat, feat), feat)
        acc[part] = jnp.dot(tok_buf[y], w_buf[part, f, :], preferred_element_type=F32)

    def token_step(i, carry):
        s, ci = i // 4 + 1, i % 4
        d, half = ci % 2, (ci + ci // 2) % 2
        slot = ring_take(tok_buf, tsend, trecv, d, half, s, jnp.logical_or(d == half, s < near))
        r = pl.ds(pl.multiple_of(half * half_rows, half_rows), half_rows)
        for part in range(3):
            acc[part, r, :] = acc[part, r, :] + project(part, slot, half)

        @pl.when(y > 0)
        def _():
            up, down = i - up_from, i - down_from
            wrapped = (z + 2 * NZ - 1 - up) % NZ >= NZ // 2

            @pl.when(i == contact_at)
            def _():
                pl.semaphore_wait(zh.at[0, 0], 1)

                @pl.when(z > 0)
                def _():
                    hello_down(0)

                @pl.when(jnp.logical_or(z == 0, z > NZ // 2))
                def _():
                    hello_up(1)

            @pl.when(jnp.logical_and(jnp.logical_and(down >= 0, down < down_rounds), z + 1 + down < NZ))
            def _():
                pl.semaphore_wait(zh.at[1, down], 1)

                @pl.when(jnp.logical_and(down + 1 < down_rounds, z > 0))
                def _():
                    hello_down(down + 1)

            @pl.when(jnp.logical_and(jnp.logical_and(up >= 1, up < up_rounds), wrapped))
            def _():
                pl.semaphore_wait(zh.at[0, up], 1)

                @pl.when(up + 1 < up_rounds)
                def _():
                    hello_up(up + 1)

            @pl.when(i == 3)
            def _():
                plane_heard(0)
                plane_hello(1)

            @pl.when(i == 5)
            def _():
                plane_heard(1)
                plane_hello(2)

            @pl.when(i == 7)
            def _():
                plane_heard(2)
                tell_first_row(0)

        return carry

    with jax.named_scope("token_ring"):
        lax.fori_loop(0, steps, token_step, 0)

    with jax.named_scope("token_last"):
        ring_take(tok_buf, tsend, trecv, 0, 0, far, None)
        slot = ring_take(tok_buf, tsend, trecv, 1, 1, far, None)
        f = pl.ds(pl.multiple_of(slot * feat, feat), feat)

        def finish(part):
            return (acc[part] + jnp.dot(tok_buf[slot], w_buf[part, f, :], preferred_element_type=F32)).astype(BF16)

    with jax.named_scope("local_state"):
        first_row_heard(0)
        for q in range(1, PLANE):
            l_copy(q).start()
        lp_buf[j] = l_send[j // 4]
        k_buf[...] = finish(1)
        v_buf[...] = finish(2)
        per = PLANE // HEADS
        seg = DH // per
        for h in range(HEADS):
            cols = slice(h * DH, (h + 1) * DH)
            weighted = (k_buf[:, cols].astype(F32) * keep_buf[h]).astype(BF16)
            local = lax.dot_general(weighted, v_buf[:, cols], (((0,), (0,)), ((), ())), preferred_element_type=F32)
            s_buf[h * per : (h + 1) * per] = local.astype(BF16).reshape(per, seg, DH)
        for q in range(1, PLANE):
            s_copy(q).start()
        sp_buf[j] = s_buf[j]

    with jax.named_scope("plane_logs"):
        tell_first_row(1)
        first_row_heard(1)
        for q in range(1, PLANE):
            l_copy(q).wait()
        total = lp_buf[0]
        for b in range(1, PLANE):
            total = total + lp_buf[b]
        lz_send[...] = total
        for k in z_order:
            @pl.when(z + k < NZ)
            def _():
                z_copy(lz_send, lz_recv, lzs, lzr, k).start()

    with jax.named_scope("intra"):
        query = finish(0)
        for h in range(HEADS):
            cols = slice(h * DH, (h + 1) * DH)
            scores = lax.dot_general(query[:, cols], k_buf[:, cols], (((1,), (1,)), ((), ())), preferred_element_type=F32)
            weights = (scores * dec_buf[h]).astype(BF16)
            intra_buf[h] = jnp.dot(weights, v_buf[:, cols], preferred_element_type=F32)

    with jax.named_scope("plane_totals"):
        for q in range(1, PLANE):
            s_copy(q).wait_recv()
        state = jnp.zeros((seg, DH), F32)
        gone = jnp.zeros((8, DH), F32)
        for b in range(PLANE):
            pre_buf[b] = state
            log_b = jnp.concatenate([lp_buf[b]] * (seg // 8), axis=0)
            state = jnp.exp(log_b) * state + sp_buf[b].astype(F32)
        t_send[...] = state.astype(BF16)
        for k in z_order:
            @pl.when(z + k < NZ)
            def _():
                z_copy(t_send, t_recv, tzs, tzr, k).start()

    with jax.named_scope("plane_weights"):
        run = jnp.zeros((8, DH), F32)
        for k in range(1, NZ):
            wz_buf[k] = jnp.exp(run)

            @pl.when(z >= k)
            def _():
                z_copy(lz_send, lz_recv, lzs, lzr, k).wait_recv()

            @pl.when(z < k)
            def _():
                lz_recv[k] = jnp.zeros((8, DH), F32)

            run = run + lz_recv[k]

    with jax.named_scope("earlier_planes"):
        pre_buf[PLANE] = jnp.zeros((seg, DH), F32)
        for k in range(1, NZ):
            @pl.when(z >= k)
            def _():
                z_copy(t_send, t_recv, tzs, tzr, k).wait_recv()
                w_k = jnp.concatenate([wz_buf[k]] * (seg // 8), axis=0)
                pre_buf[PLANE] = pre_buf[PLANE] + w_k * t_recv[k].astype(F32)

    with jax.named_scope("prefixes"):
        before = pre_buf[PLANE]
        for b in range(PLANE):
            gone_b = jnp.concatenate([jnp.exp(gone)] * (seg // 8), axis=0)
            st_send[b] = (gone_b * before + pre_buf[b]).astype(BF16)
            gone = gone + lp_buf[b]
        for q in range(1, PLANE):
            st_copy(q).start()
        st_recv[j] = st_send[j]
        for q in range(1, PLANE):
            st_copy(q).wait_recv()

    with jax.named_scope("normed"):
        for half in range(2):
            r = slice(half * half_rows, (half + 1) * half_rows)
            for h in range(HEADS):
                cols = slice(h * DH, (h + 1) * DH)
                prev = st_recv[h * per : (h + 1) * per].reshape(DH, DH)
                inter = jnp.dot(query[r, cols], prev, preferred_element_type=F32) * eb_buf[h, r, :]
                attn = intra_buf[h, r, :] + inter
                normed = attn * lax.rsqrt(jnp.mean(attn * attn, axis=1, keepdims=True) + 1e-6)
                n_buf[y, r, cols] = normed.astype(BF16)
            for d in (half, 1 - half):
                if d == half or near > 0:
                    for q in range(2):
                        ring_copy(n_buf.at[y], n_buf, nsend, nrecv, d, half, 0, y, q).start()

    width = HEADS * DH
    wout_copy.wait()
    f = pl.ds(pl.multiple_of(y * width, width), width)
    oacc[...] = jnp.dot(n_buf[y], wout_buf[f, :], preferred_element_type=F32)

    def out_step(i, carry):
        s, ci = i // 4 + 1, i % 4
        d, half = ci % 2, (ci + ci // 2) % 2
        slot = ring_take(n_buf, nsend, nrecv, d, half, s, jnp.logical_or(d == half, s < near))
        r = pl.ds(pl.multiple_of(half * half_rows, half_rows), half_rows)
        f = pl.ds(pl.multiple_of(slot * width, width), width)
        oacc[r, :] = oacc[r, :] + jnp.dot(n_buf[slot, r, :], wout_buf[f, :], preferred_element_type=F32)
        return carry

    with jax.named_scope("out_ring"):
        lax.fori_loop(0, steps, out_step, 0)
    with jax.named_scope("out_last"):
        ring_take(n_buf, nsend, nrecv, 0, 0, far, None)
        slot = ring_take(n_buf, nsend, nrecv, 1, 1, far, None)
        f = pl.ds(pl.multiple_of(slot * width, width), width)
        out_ref[...] = (oacc[...] + jnp.dot(n_buf[slot], wout_buf[f, :], preferred_element_type=F32)).astype(BF16)

    with jax.named_scope("drain"):
        ring_drain(tok_hbm, tok_buf, tsend, trecv)
        ring_drain(n_buf.at[y], n_buf, nsend, nrecv)
        for q in range(1, PLANE):
            s_copy(q).wait_send()
            st_copy(q).wait_send()
        for k in range(1, NZ):
            @pl.when(z + k < NZ)
            def _():
                z_copy(lz_send, lz_recv, lzs, lzr, k).wait_send()
                z_copy(t_send, t_recv, tzs, tzr, k).wait_send()


def body(NY, NZ, tokens, w_qkv, log_gate, w_out):
    rows, feat = tokens.shape
    width = HEADS * DH
    seg = HEADS * DH // PLANE
    dma = pltpu.SemaphoreType.DMA
    far = NY // 2
    any_spec = pl.BlockSpec(memory_space=pl.ANY)
    vmem_spec = pl.BlockSpec(memory_space=pltpu.VMEM)
    w3 = jnp.transpose(w_qkv, (1, 0, 2))
    gates = jnp.transpose(log_gate, (1, 0))
    scratch = [
        pltpu.VMEM((NY, rows, feat), BF16),
        pltpu.VMEM(w3.shape, BF16),
        pltpu.VMEM(w_out.shape, BF16),
        pltpu.VMEM((3, rows, width), F32),
        pltpu.VMEM((rows, width), BF16),
        pltpu.VMEM((rows, width), BF16),
        pltpu.VMEM((HEADS, rows, rows), F32),
        pltpu.VMEM((HEADS, rows, DH), F32),
        pltpu.VMEM((HEADS, rows, DH), F32),
        pltpu.VMEM((HEADS, rows, DH), F32),
        pltpu.VMEM((NY, rows, width), BF16),
        pltpu.VMEM((rows, w_out.shape[1]), F32),
        pltpu.VMEM((PLANE, seg, DH), BF16),
        pltpu.VMEM((PLANE, seg, DH), BF16),
        pltpu.VMEM((PLANE + 1, seg, DH), F32),
        pltpu.VMEM((seg, DH), BF16),
        pltpu.VMEM((NZ, seg, DH), BF16),
        pltpu.VMEM((PLANE, seg, DH), BF16),
        pltpu.VMEM((PLANE, seg, DH), BF16),
        pltpu.VMEM((HEADS, 8, DH), F32),
        pltpu.VMEM((PLANE, 8, DH), F32),
        pltpu.VMEM((8, DH), F32),
        pltpu.VMEM((NZ, 8, DH), F32),
        pltpu.VMEM((NZ, 8, DH), F32),
        dma, dma, dma,
        dma((2, 2, far, 2)), dma((2, 2, far, 2)), dma((2, 2, far, 2)), dma((2, 2, far, 2)),
        pltpu.SemaphoreType.REGULAR((2, NZ // 2)),
        pltpu.SemaphoreType.REGULAR((3, 3)),
        pltpu.SemaphoreType.REGULAR((2,)),
        dma((PLANE,)), dma((PLANE,)),
        dma((NZ,)), dma((NZ,)),
        dma((PLANE,)), dma((PLANE,)),
        dma((NZ,)), dma((NZ,)),
        dma((PLANE,)), dma((PLANE,)),
    ]
    return pl.pallas_call(
        functools.partial(kernel, NY, NZ),
        out_shape=jax.ShapeDtypeStruct((rows, w_out.shape[1]), BF16),
        in_specs=[any_spec, any_spec, vmem_spec, any_spec],
        out_specs=vmem_spec,
        scratch_shapes=scratch,
        compiler_params=pltpu.CompilerParams(
            collective_id=0, has_side_effects=True, vmem_limit_bytes=63 << 20
        ),
    )(tokens, w3, gates, w_out)


def solution(mesh):
    placed = (P("ctx", "head"), P(None, None, "head"), P("ctx", "head"), P(None, "head"))
    return jax.shard_map(
        functools.partial(body, mesh.shape["head"], mesh.shape["ctx"] // PLANE),
        mesh=mesh, in_specs=placed, out_specs=P("ctx", "head"), check_vma=False,
    )
```
